32 devices in a mesh: seq: 8 (over z, y), head: 4 (over x, core).
Axes of the slice: x: 2, y: 2, z: 4, core: 2. Of those that a mesh axis runs over, the one named last changes fastest.
Arguments:
- queries: float32 [1024, 2048], P('seq', 'head'), may hold values from -6 to 6
- keys: float32 [1024, 2048], P('seq', 'head'), may hold values from -6 to 6
- values: float32 [1024, 2048], P('seq', 'head'), may hold values from -6 to 6
- rates: float32 [4, 1024], P('head', 'seq'), may hold values from 0.05 to 1
- gate_fast: float32 [4, 512, 512], P('head'), may hold values from -0.25 to 0.25
- up_fast: float32 [4, 512, 512], P('head'), may hold values from -0.25 to 0.25
- down_fast: float32 [4, 512, 512], P('head'), may hold values from -0.25 to 0.25
- out_proj: bfloat16 [2048, 4096], P('head', 'seq'), may hold values from -0.125 to 0.125
- out_grad: bfloat16 [1024, 4096], P('seq', 'head'), may hold values from -6 to 6
Outputs:
- query_grad: float32 [1024, 2048], P('seq', 'head')
- key_grad: float32 [1024, 2048], P('seq', 'head')
- value_grad: float32 [1024, 2048], P('seq', 'head')
- gate_grad: float32 [4, 512, 512], P('head', 'seq')
- up_grad: float32 [4, 512, 512], P('head', 'seq')
- down_grad: float32 [4, 512, 512], P('head', 'seq')
The draws below stay inside these ranges and needn't reach their ends.
All inputs are finite; a program needn't handle non-finite values.
Results may differ from the reference program's by a relative error of at most 0.0003.
Values may be sent and summed in bfloat16 or wider, within the bound.
No kernel may reach another device: no remote copies, remote signals or barrier semaphores. Data moves between devices by JAX's collectives and lax.ppermute only.
A program may use at most 64 MiB of HBM per device.

```python
import math
import jax
import jax.numpy as jnp
from jax import lax

D = 4096
HEAD_DIM = 512
FAST_FF = 512
HEADS = 4
GROUP = 1024


def block_scale(own_key, shape, pieces, low, top_value):
    def one(dim, shards_of):
        heights = jax.random.uniform(jax.random.fold_in(jax.random.fold_in(own_key, 6), dim), (shards_of,), jnp.float32, low / len(pieces), top_value / len(pieces))
        return jnp.repeat(jnp.exp(heights), shape[dim] // shards_of).reshape((-1,) + (1,) * (len(shape) - dim - 1))

    gain = one(*pieces[0])
    for cut in pieces[1:]:
        gain = gain * one(*cut)
    return gain


def noise(rng, shape, width, limit, split=(), held_as=jnp.bfloat16):
    values = width * jax.random.normal(rng, shape, jnp.float32)
    if split:
        values = values * block_scale(rng, shape, split, -0.22, 0.18)
    return jnp.clip(values, -limit, limit).astype(held_as)


def setup_inputs(seed: int = 0) -> dict:
    seeds = jax.random.split(jax.random.key(seed), 10)
    return {
        "queries": noise(seeds[0], (GROUP, HEADS * HEAD_DIM), 1.0, 6.0, ((0, 8), (1, 4)), jnp.float32),
        "keys": noise(seeds[1], (GROUP, HEADS * HEAD_DIM), 1.0, 6.0, ((0, 8), (1, 4)), jnp.float32),
        "values": noise(seeds[2], (GROUP, HEADS * HEAD_DIM), 1.0, 6.0, ((0, 8), (1, 4)), jnp.float32),
        "rates": jnp.clip(jnp.exp(math.log(1.0) - 2.9957323 * jax.random.uniform(seeds[3], (HEADS, GROUP), jnp.float32) ** block_scale(seeds[3], (HEADS, GROUP), ((0, 4), (1, 8)), -0.2, 0.2)), 0.05, 1.0),
        "gate_fast": noise(seeds[4], (HEADS, FAST_FF, HEAD_DIM), HEAD_DIM ** -0.5, 0.25, ((0, 4),), jnp.float32),
        "up_fast": noise(seeds[5], (HEADS, FAST_FF, HEAD_DIM), HEAD_DIM ** -0.5, 0.25, ((0, 4),), jnp.float32),
        "down_fast": noise(seeds[6], (HEADS, HEAD_DIM, FAST_FF), FAST_FF ** -0.5, 0.25, ((0, 4),), jnp.float32),
        "out_proj": noise(seeds[7], (HEADS * HEAD_DIM, D), (HEADS * HEAD_DIM) ** -0.5, 0.125, ((0, 4), (1, 8))),
        "out_grad": noise(seeds[8], (GROUP, D), 1.0, 6.0, ((0, 8), (1, 4))),
    }


def matmul(left, right):
    return jnp.dot(left, right, precision=lax.Precision.HIGHEST, preferred_element_type=jnp.float32)

def swiglu(gate_matrix, up_matrix, down_matrix, inputs):
    before = matmul(inputs, gate_matrix.T)
    linear = matmul(inputs, up_matrix.T)
    hidden = jax.nn.silu(before) * linear
    return matmul(hidden, down_matrix.T)

def update_terms(gate_matrix, up_matrix, down_matrix, key_rows, value_rows, rate_rows):
    before = matmul(key_rows, gate_matrix.T)
    linear = matmul(key_rows, up_matrix.T)
    sigma = jax.nn.sigmoid(before)
    activated = before * sigma
    hidden = activated * linear
    target = -(rate_rows[:, None] * value_rows)
    term_down = matmul(target.T, hidden)
    hidden_grad = matmul(target, down_matrix)
    before_grad = hidden_grad * linear * sigma * (1.0 + before * (1.0 - sigma))
    linear_grad = hidden_grad * activated
    return (matmul(before_grad.T, key_rows), matmul(linear_grad.T, key_rows), term_down)

def renorm(weight, partial_value, total_sq, scale):
    norm_update = jnp.sqrt(total_sq + 1e-06)
    moved = weight - partial_value * (scale / norm_update)[..., None, None]
    norm_old = jnp.sqrt(lax.optimization_barrier(jnp.sum(weight * weight, axis=-1)) + 1e-06)
    norm_new = jnp.sqrt(lax.optimization_barrier(jnp.sum(moved * moved, axis=-1)) + 1e-06)
    return (moved * (norm_old / norm_new)[..., None], norm_new, norm_update)

def back_rows(weight, renormed, norm_new, grad, norm_update, scale):
    norm_old = jnp.sqrt(lax.optimization_barrier(jnp.sum(weight * weight, axis=-1)) + 1e-06)
    moved = renormed * (norm_new / norm_old)[..., None]
    partial_value = (weight - moved) * (norm_update / scale)[..., None, None]
    along = lax.optimization_barrier(jnp.sum(moved * grad, axis=-1))
    moved_grad = (norm_old / norm_new)[..., None] * (grad - moved * (along / (norm_new * norm_new))[..., None])
    direct = moved_grad + (along / (norm_new * norm_old))[..., None] * weight
    return (direct, -moved_grad, partial_value)

def step_back(step_grad, partial_value, inner, norm_update, scale):
    factor = inner / (norm_update * norm_update)
    return (scale / norm_update)[..., None, None] * (step_grad - partial_value * factor[..., None, None])

def reference(queries, keys, values, rates, gate_fast, up_fast, down_fast, out_proj, out_grad):
    head_size = gate_fast.shape[2]
    out_cot = jnp.dot(out_grad, out_proj.T, preferred_element_type=jnp.float32)
    query_list, key_list, value_list = ([], [], [])
    gate_list, up_list, down_list = ([], [], [])
    for member in range(gate_fast.shape[0]):
        lower = member * head_size
        upper = lower + head_size
        weights = (gate_fast[member], up_fast[member], down_fast[member])
        scales = tuple((0.3 * math.sqrt(matrix.shape[0]) for matrix in weights))
        rate_rows = rates[member]

        def update_of(gate_matrix, up_matrix, down_matrix, key_rows, value_rows):
            return update_terms(gate_matrix, up_matrix, down_matrix, key_rows, value_rows, rate_rows)
        partials, update_pull = jax.vjp(update_of, weights[0], weights[1], weights[2], keys[:, lower:upper], values[:, lower:upper])
        normed = [renorm(weights[slot], partials[slot], jnp.sum(partials[slot] * partials[slot]), scales[slot]) for slot in range(3)]
        applied, apply_pull = jax.vjp(swiglu, normed[0][0], normed[1][0], normed[2][0], queries[:, lower:upper])
        cot_gate, cot_up, cot_down, query_part = apply_pull(out_cot[:, lower:upper])
        cots = (cot_gate, cot_up, cot_down)
        directs, directions = ([], [])
        for slot in range(3):
            direct, step_grad, partial_value = back_rows(weights[slot], normed[slot][0], normed[slot][1], cots[slot], normed[slot][2], scales[slot])
            inner = jnp.sum(partial_value * step_grad)
            directs.append(direct)
            directions.append(step_back(step_grad, partial_value, inner, normed[slot][2], scales[slot]))
        through_gate, through_up, through_down, key_part, value_part = update_pull((directions[0], directions[1], directions[2]))
        query_list.append(query_part)
        key_list.append(key_part)
        value_list.append(value_part)
        gate_list.append(directs[0] + through_gate)
        up_list.append(directs[1] + through_up)
        down_list.append(directs[2] + through_down)
    return (jnp.concatenate(query_list, axis=1), jnp.concatenate(key_list, axis=1), jnp.concatenate(value_list, axis=1), jnp.stack(gate_list), jnp.stack(up_list), jnp.stack(down_list))
```

```python
import math

import jax
import jax.numpy as jnp
from jax import lax
from jax.sharding import PartitionSpec as P


def matmul(left, right):
    return jnp.dot(left, right, precision=lax.Precision.HIGHEST, preferred_element_type=jnp.float32)


def swiglu(gate_matrix, up_matrix, down_matrix, inputs):
    before = matmul(inputs, gate_matrix.T)
    linear = matmul(inputs, up_matrix.T)
    hidden = jax.nn.silu(before) * linear
    return matmul(hidden, down_matrix.T)


def update_terms(gate_matrix, up_matrix, down_matrix, key_rows, value_rows, rate_rows):
    before = matmul(key_rows, gate_matrix.T)
    linear = matmul(key_rows, up_matrix.T)
    sigma = jax.nn.sigmoid(before)
    activated = before * sigma
    hidden = activated * linear
    target = -(rate_rows[:, None] * value_rows)
    term_down = matmul(target.T, hidden)
    hidden_grad = matmul(target, down_matrix)
    before_grad = hidden_grad * linear * sigma * (1.0 + before * (1.0 - sigma))
    linear_grad = hidden_grad * activated
    return (matmul(before_grad.T, key_rows), matmul(linear_grad.T, key_rows), term_down)


def renorm(weight, partial_value, total_sq, scale):
    norm_update = jnp.sqrt(total_sq + 1e-06)
    moved = weight - partial_value * (scale / norm_update)[..., None, None]
    norm_old = jnp.sqrt(jnp.sum(weight * weight, axis=-1) + 1e-06)
    norm_new = jnp.sqrt(jnp.sum(moved * moved, axis=-1) + 1e-06)
    return (moved * (norm_old / norm_new)[..., None], norm_new, norm_update)


def back_rows(weight, renormed, norm_new, grad, norm_update, scale):
    norm_old = jnp.sqrt(jnp.sum(weight * weight, axis=-1) + 1e-06)
    moved = renormed * (norm_new / norm_old)[..., None]
    partial_value = (weight - moved) * (norm_update / scale)[..., None, None]
    along = jnp.sum(moved * grad, axis=-1)
    moved_grad = (norm_old / norm_new)[..., None] * (
        grad - moved * (along / (norm_new * norm_new))[..., None]
    )
    direct = moved_grad + (along / (norm_new * norm_old))[..., None] * weight
    return (direct, -moved_grad, partial_value)


def step_back(step_grad, partial_value, inner, norm_update, scale):
    factor = inner / (norm_update * norm_update)
    return (scale / norm_update)[..., None, None] * (
        step_grad - partial_value * factor[..., None, None]
    )


def body(queries, keys, values, rates, gate_fast, up_fast, down_fast, out_proj, out_grad):
    tokens_here = queries.shape[0]
    heads_here = gate_fast.shape[0]
    head_size = gate_fast.shape[2]
    seq_count = lax.axis_size("seq")
    seq_index = lax.axis_index("seq")

    def split_heads(array):
        return array.reshape(tokens_here, heads_here, head_size).transpose(1, 0, 2)

    def join_heads(array):
        return array.transpose(1, 0, 2).reshape(tokens_here, heads_here * head_size)

    grad_full = lax.all_gather(out_grad, "head", axis=1, tiled=True)
    out_cot = lax.dot_general(
        grad_full,
        lax.all_gather(out_proj, "seq", axis=1, tiled=True),
        (((1,), (1,)), ((), ())),
        preferred_element_type=jnp.float32,
    )
    weights = (gate_fast, up_fast, down_fast)
    scales = tuple((0.3 * math.sqrt(matrix.shape[1]) for matrix in weights))
    share_rows = [matrix.shape[1] // seq_count for matrix in weights]

    def update_heads(gate_matrix, up_matrix, down_matrix, key_heads, value_heads):
        return jax.vmap(update_terms)(
            gate_matrix, up_matrix, down_matrix, key_heads, value_heads, rates
        )

    partials, update_pull = jax.vjp(
        update_heads, gate_fast, up_fast, down_fast, split_heads(keys), split_heads(values)
    )
    totals = lax.psum((partials[0], partials[1], partials[2]), "seq")
    normed = [
        renorm(
            weights[slot],
            totals[slot],
            jnp.sum(totals[slot] * totals[slot], axis=(1, 2)),
            scales[slot],
        )
        for slot in range(3)
    ]
    renormed = [normed[slot][0] for slot in range(3)]
    new_norms = [normed[slot][1] for slot in range(3)]
    update_norms = [normed[slot][2] for slot in range(3)]

    def apply_heads(gate_matrix, up_matrix, down_matrix, query_heads):
        return jax.vmap(swiglu)(gate_matrix, up_matrix, down_matrix, query_heads)

    applied, apply_pull = jax.vjp(
        apply_heads, renormed[0], renormed[1], renormed[2], split_heads(queries)
    )
    cot_gate, cot_up, cot_down, query_part = apply_pull(split_heads(out_cot))
    summed = lax.psum((cot_gate, cot_up, cot_down), "seq")
    backs = [
        back_rows(
            weights[slot],
            renormed[slot],
            new_norms[slot],
            summed[slot],
            update_norms[slot],
            scales[slot],
        )
        for slot in range(3)
    ]
    directions = [
        step_back(
            backs[slot][1],
            backs[slot][2],
            jnp.sum(backs[slot][2] * backs[slot][1], axis=(1, 2)),
            update_norms[slot],
            scales[slot],
        )
        for slot in range(3)
    ]
    directs = [
        lax.dynamic_slice_in_dim(backs[slot][0], seq_index * share_rows[slot], share_rows[slot], 1)
        for slot in range(3)
    ]
    through_gate, through_up, through_down, key_part, value_part = update_pull(
        (directions[0], directions[1], directions[2])
    )
    throughs = (
        lax.psum_scatter(through_gate, "seq", scatter_dimension=1, tiled=True),
        lax.psum_scatter(through_up, "seq", scatter_dimension=1, tiled=True),
        lax.psum_scatter(through_down, "seq", scatter_dimension=1, tiled=True),
    )
    return (
        join_heads(query_part),
        join_heads(key_part),
        join_heads(value_part),
        directs[0] + throughs[0],
        directs[1] + throughs[1],
        directs[2] + throughs[2],
    )


LEVELS = 31000.0
CODE_BASE = 120.0


def matmul3(left, right, dims):
    return lax.dot_general(
        left, right, (dims, ((), ())), precision=lax.Precision.HIGH, preferred_element_type=jnp.float32
    )


def nt(left, right):
    return matmul3(left, right, ((1,), (1,)))


def nn(left, right):
    return matmul3(left, right, ((1,), (0,)))


def tn(left, right):
    return matmul3(left, right, ((0,), (0,)))


def encode(rows):
    top = jnp.max(jnp.abs(rows), axis=1, keepdims=True)
    scale = lax.reduce_precision(top * 1.01 + 1e-30, 8, 7)
    level = jnp.abs(rows) * (LEVELS / 128.0 / scale)
    power = jnp.floor(level)
    code = jnp.exp2(power - CODE_BASE) * (1.0 + (level - power))
    return jnp.where(rows < 0, -code, code).astype(jnp.bfloat16), scale.astype(jnp.bfloat16)


def decode(codes, scale):
    codes = codes.astype(jnp.float32)
    size = jnp.abs(codes)
    power = jnp.floor(jnp.log2(size))
    level = (power + CODE_BASE) + (size * jnp.exp2(-power) - 1.0)
    level = level * (scale.astype(jnp.float32) * (128.0 / LEVELS))
    return jnp.where(codes < 0, -level, level)


def pack(*parts):
    width = 128 // len(parts)
    coded = [encode(part) for part in parts]
    spread = [jnp.broadcast_to(scale, (scale.shape[0], width)) for _, scale in coded]
    return jnp.concatenate([codes for codes, _ in coded] + spread, axis=1)


def unpack(packed, count):
    width = 128 // count
    size = (packed.shape[1] - 128) // count
    return tuple(
        decode(
            packed[:, slot * size : (slot + 1) * size],
            packed[:, count * size + slot * width : count * size + slot * width + 1],
        )
        for slot in range(count)
    )


def silu_parts(before):
    sigma = jax.nn.sigmoid(before)
    return sigma, before * sigma, sigma * (1.0 + before * (1.0 - sigma))


def body_hidden(queries, keys, values, rates, gate_fast, up_fast, down_fast, out_proj, out_grad):
    heads = lax.axis_size("head")
    seq_count = lax.axis_size("seq")
    depth = seq_count // 2
    place = lax.axis_index("seq")
    along_z = place // 2
    along_y = place % 2
    head_size = gate_fast.shape[2]
    hidden_size = gate_fast.shape[1]
    part = hidden_size // depth
    tokens = queries.shape[0]

    def turn(array, step):
        perm = [(s, (s + 2 * step) % seq_count) for s in range(seq_count)]
        return lax.ppermute(array, "seq", perm)

    def swap(array):
        return lax.ppermute(array, "seq", [(s, s ^ 1) for s in range(seq_count)])

    def gather_z(packed):
        return [turn(packed, step) for step in range(1, depth)]

    def scatter_z(slots, *more):
        groups = (slots,) + more
        sent = [
            turn(pack(*(group[step * tokens : (step + 1) * tokens] for group in groups)), -step)
            for step in range(1, depth)
        ]
        sums = [group[:tokens] for group in groups]
        for packed in sent:
            sums = [total + piece for total, piece in zip(sums, unpack(packed, len(groups)))]
        return sums

    def sum_z(array):
        total = array
        for step in range(1, depth):
            total = total + turn(array, step)
        return total

    quarter = tokens // heads
    og_parts = []
    for step in range(depth):
        perm = []
        for s in range(seq_count):
            for h in range(heads):
                dest = (s // 2 + step) % heads
                perm.append((s * heads + h, (2 * h + s % 2) * heads + dest))
        chosen = lax.dynamic_slice_in_dim(out_grad, ((along_z + step) % heads) * quarter, quarter, 0)
        og_parts.append(lax.ppermute(chosen, ("seq", "head"), perm))
    my_head = lax.axis_index("head")
    target = -(rates[0][:, None] * values)
    kv_sent = gather_z(pack(keys, target))
    op_other = swap(out_proj)
    op_mine = jnp.where(along_y == 0, jnp.concatenate([out_proj, op_other], 1), jnp.concatenate([op_other, out_proj], 1))
    og_mine = jnp.stack(og_parts, axis=0)

    def head_turn(array, step):
        return lax.ppermute(array, "head", [(h, (h + step) % heads) for h in range(heads)])

    og_all = [og_mine] + [head_turn(og_mine, step) for step in range(1, heads)]
    og_all = jnp.stack(og_all, axis=0)
    quarters = (my_head - jnp.arange(heads)) % heads
    slots = []
    for j in range(depth):
        rows = []
        for q in range(heads):
            k = (my_head - q) % heads
            step = (q - (along_z - j)) % depth
            rows.append(lax.dynamic_slice(og_all, (k, step, 0, 0), (1, 1) + og_all.shape[2:])[0, 0])
        slots.append(jnp.concatenate(rows, axis=0))
    og_rows = jnp.concatenate(slots, axis=0)
    out_part = lax.dot_general(og_rows, op_mine, (((1,), (1,)), ((), ())), preferred_element_type=jnp.float32)
    q_sent = gather_z(pack(queries))
    (out_cot,) = scatter_z(out_part)
    oc_sent = gather_z(pack(out_cot))

    start = along_z * part
    gate = lax.dynamic_slice_in_dim(gate_fast[0], start, part, 0)
    up = lax.dynamic_slice_in_dim(up_fast[0], start, part, 0)
    down = lax.dynamic_slice_in_dim(down_fast[0], start, part, 1).T
    weights = (gate, up, down)
    scales = tuple(
        0.3 * math.sqrt(matrix.shape[1]) for matrix in (gate_fast, up_fast, down_fast)
    )
    old_gate = jnp.sqrt(jnp.sum(gate * gate, axis=1, keepdims=True) + 1e-06)
    old_up = jnp.sqrt(jnp.sum(up * up, axis=1, keepdims=True) + 1e-06)
    down_sq = jnp.sum(down_fast[0] * down_fast[0], axis=1)[None, :]
    old_down = jnp.sqrt(down_sq + 1e-06)

    kv_parts = [unpack(packed, 2) for packed in kv_sent]
    key_rows = jnp.concatenate([keys] + [pair[0] for pair in kv_parts], axis=0)
    target_rows = jnp.concatenate([target] + [pair[1] for pair in kv_parts], axis=0)

    before = nt(key_rows, gate)
    linear = nt(key_rows, up)
    hgrad = nt(target_rows, down)
    sigma, act, slope = silu_parts(before)
    hidden = act * linear
    bgrad = hgrad * linear * slope
    lgrad = hgrad * act
    partial = jnp.stack([tn(bgrad, key_rows), tn(lgrad, key_rows), tn(hidden, target_rows)])
    partial = partial + swap(partial)

    def lanes(vector):
        return vector.reshape(-1, 128)

    def sums_of(first, second, third, rows_first, rows_second):
        blocks = [
            jnp.full((1, 128), first),
            jnp.full((1, 128), second),
            jnp.full((1, 128), third),
            lanes(rows_first),
            lanes(rows_second),
        ]
        total = sum_z(jnp.concatenate(blocks, axis=0))
        count = head_size // 128
        return (
            total[0, 0],
            total[1, 0],
            total[2, 0],
            total[3 : 3 + count].reshape(1, head_size),
            total[3 + count : 3 + 2 * count].reshape(1, head_size),
        )

    sq_rows = jnp.sum(partial[2] * partial[2], axis=0)
    gate_sq, up_sq, down_total, sq_down, cross_down = sums_of(
        jnp.sum(partial[0] * partial[0]),
        jnp.sum(partial[1] * partial[1]),
        jnp.sum(sq_rows),
        sq_rows,
        jnp.sum(partial[2] * down, axis=0),
    )
    norms = [jnp.sqrt(value + 1e-06) for value in (gate_sq, up_sq, down_total)]
    moved = [weights[slot] - partial[slot] * (scales[slot] / norms[slot]) for slot in range(3)]
    ratio = scales[2] / norms[2]
    new_down_sq = jnp.maximum(down_sq - 2.0 * ratio * cross_down + ratio * ratio * sq_down, 0.0)
    new_norms = [
        jnp.sqrt(jnp.sum(moved[0] * moved[0], axis=1, keepdims=True) + 1e-06),
        jnp.sqrt(jnp.sum(moved[1] * moved[1], axis=1, keepdims=True) + 1e-06),
        jnp.sqrt(new_down_sq + 1e-06),
    ]
    old_norms = [old_gate, old_up, old_down]
    renormed = [moved[slot] * (old_norms[slot] / new_norms[slot]) for slot in range(3)]

    query_rows = jnp.concatenate([queries] + [unpack(packed, 1)[0] for packed in q_sent], axis=0)
    cot_rows = jnp.concatenate([out_cot] + [unpack(packed, 1)[0] for packed in oc_sent], axis=0)
    q_before = nt(query_rows, renormed[0])
    q_linear = nt(query_rows, renormed[1])
    _, q_act, q_slope = silu_parts(q_before)
    q_hidden = q_act * q_linear
    h_cot = nt(cot_rows, renormed[2])
    b_cot = h_cot * q_linear * q_slope
    l_cot = h_cot * q_act
    cots = jnp.stack([tn(b_cot, query_rows), tn(l_cot, query_rows), tn(q_hidden, cot_rows)])
    cots = cots + swap(cots)
    query_part = nn(b_cot, renormed[0]) + nn(l_cot, renormed[1])
    (query_grad,) = scatter_z(query_part)

    along_gate = jnp.sum(moved[0] * cots[0], axis=1, keepdims=True)
    along_up = jnp.sum(moved[1] * cots[1], axis=1, keepdims=True)

    def step_of(slot, along):
        return (old_norms[slot] / new_norms[slot]) * (
            cots[slot] - moved[slot] * (along / (new_norms[slot] * new_norms[slot]))
        )

    moved_grads = [step_of(0, along_gate), step_of(1, along_up)]
    inner_gate, inner_up, _, along_down, dot_down = sums_of(
        -jnp.sum(partial[0] * moved_grads[0]),
        -jnp.sum(partial[1] * moved_grads[1]),
        0.0,
        jnp.sum(moved[2] * cots[2], axis=0),
        jnp.sum(partial[2] * cots[2], axis=0),
    )
    moved_grads.append(step_of(2, along_down))
    moved_dot = cross_down - ratio * sq_down
    inner_down = -jnp.sum(
        (old_norms[2] / new_norms[2])
        * (dot_down - moved_dot * (along_down / (new_norms[2] * new_norms[2])))
    )
    alongs = (along_gate, along_up, along_down)
    inners = (inner_gate, inner_up, inner_down)
    directs = [
        moved_grads[slot] + (alongs[slot] / (new_norms[slot] * old_norms[slot])) * weights[slot]
        for slot in range(3)
    ]
    directions = [
        (scales[slot] / norms[slot])
        * (-moved_grads[slot] - partial[slot] * (inners[slot] / (norms[slot] * norms[slot])))
        for slot in range(3)
    ]

    c_bgrad = nt(key_rows, directions[0])
    c_lgrad = nt(key_rows, directions[1])
    c_hidden = nt(target_rows, directions[2])
    bend = sigma * (1.0 - sigma) * (2.0 + before * (1.0 - 2.0 * sigma))
    c_linear = c_hidden * act + c_bgrad * hgrad * slope
    c_hgrad = c_bgrad * linear * slope + c_lgrad * act
    c_before = c_hidden * linear * slope + c_bgrad * hgrad * linear * bend + c_lgrad * hgrad * slope
    key_part = nn(
        jnp.concatenate([bgrad, lgrad, c_before, c_linear], axis=1),
        jnp.concatenate([directions[0], directions[1], gate, up], axis=0),
    )
    target_part = nn(
        jnp.concatenate([hidden, c_hgrad], axis=1), jnp.concatenate([directions[2], down], axis=0)
    )
    key_grad, target_grad = scatter_z(key_part, target_part)
    value_grad = -(rates[0][:, None] * target_grad)

    half = part // 2
    through = jnp.stack([tn(c_before, key_rows), tn(c_linear, key_rows)])
    direct_half = jnp.stack(directs[:2])
    mine = lax.dynamic_slice_in_dim(through + direct_half, along_y * half, half, 1)
    other = lax.dynamic_slice_in_dim(through, (1 - along_y) * half, half, 1)
    rows_out = mine + swap(other)
    down_part = tn(target_rows, c_hgrad) + jnp.where(along_y == 0, directs[2].T, 0.0)
    share = head_size // seq_count
    down_all = lax.all_to_all(down_part, "seq", 0, 0, tiled=True)
    down_all = down_all.reshape(depth, 2, share, part).sum(axis=1)
    down_out = down_all.transpose(1, 0, 2).reshape(share, hidden_size)
    return (query_grad, key_grad, value_grad, rows_out[0][None], rows_out[1][None], down_out[None])


def fits_hidden(mesh, tokens, hidden, head_size, heads):
    seq_count = mesh.shape["seq"]
    head_count = mesh.shape["head"]
    return (
        seq_count == 2 * head_count
        and heads == head_count
        and tokens <= 3 * hidden
        and hidden % (seq_count * 16) == 0
        and head_size % 128 == 0
        and tokens % (seq_count * head_count * 16) == 0
    )


def solution(mesh):
    placed = (
        P("seq", "head"),
        P("seq", "head"),
        P("seq", "head"),
        P("head", "seq"),
        P("head", None, None),
        P("head", None, None),
        P("head", None, None),
        P("head", "seq"),
        P("seq", "head"),
    )
    outs = (
        P("seq", "head"),
        P("seq", "head"),
        P("seq", "head"),
        P("head", "seq", None),
        P("head", "seq", None),
        P("head", "seq", None),
    )

    def whole(*arrays):
        hidden, head_size = arrays[4].shape[1:]
        small = fits_hidden(mesh, arrays[0].shape[0], hidden, head_size, arrays[4].shape[0])
        chosen = body_hidden if small else body
        return jax.shard_map(chosen, mesh=mesh, in_specs=placed, out_specs=outs, check_vma=False)(*arrays)

    return whole
```

```python
import math

import jax
import jax.numpy as jnp
from jax import lax
from jax.experimental import pallas as pl
from jax.experimental.pallas import tpu as pltpu
from jax.sharding import PartitionSpec as P


def matmul(left, right):
    return jnp.dot(left, right, precision=lax.Precision.HIGHEST, preferred_element_type=jnp.float32)


def swiglu(gate_matrix, up_matrix, down_matrix, inputs):
    before = matmul(inputs, gate_matrix.T)
    linear = matmul(inputs, up_matrix.T)
    hidden = jax.nn.silu(before) * linear
    return matmul(hidden, down_matrix.T)


def update_terms(gate_matrix, up_matrix, down_matrix, key_rows, value_rows, rate_rows):
    before = matmul(key_rows, gate_matrix.T)
    linear = matmul(key_rows, up_matrix.T)
    sigma = jax.nn.sigmoid(before)
    activated = before * sigma
    hidden = activated * linear
    target = -(rate_rows[:, None] * value_rows)
    term_down = matmul(target.T, hidden)
    hidden_grad = matmul(target, down_matrix)
    before_grad = hidden_grad * linear * sigma * (1.0 + before * (1.0 - sigma))
    linear_grad = hidden_grad * activated
    return (matmul(before_grad.T, key_rows), matmul(linear_grad.T, key_rows), term_down)


def renorm(weight, partial_value, total_sq, scale):
    norm_update = jnp.sqrt(total_sq + 1e-06)
    moved = weight - partial_value * (scale / norm_update)[..., None, None]
    norm_old = jnp.sqrt(jnp.sum(weight * weight, axis=-1) + 1e-06)
    norm_new = jnp.sqrt(jnp.sum(moved * moved, axis=-1) + 1e-06)
    return (moved * (norm_old / norm_new)[..., None], norm_new, norm_update)


def back_rows(weight, renormed, norm_new, grad, norm_update, scale):
    norm_old = jnp.sqrt(jnp.sum(weight * weight, axis=-1) + 1e-06)
    moved = renormed * (norm_new / norm_old)[..., None]
    partial_value = (weight - moved) * (norm_update / scale)[..., None, None]
    along = jnp.sum(moved * grad, axis=-1)
    moved_grad = (norm_old / norm_new)[..., None] * (
        grad - moved * (along / (norm_new * norm_new))[..., None]
    )
    direct = moved_grad + (along / (norm_new * norm_old))[..., None] * weight
    return (direct, -moved_grad, partial_value)


def step_back(step_grad, partial_value, inner, norm_update, scale):
    factor = inner / (norm_update * norm_update)
    return (scale / norm_update)[..., None, None] * (
        step_grad - partial_value * factor[..., None, None]
    )


def body(queries, keys, values, rates, gate_fast, up_fast, down_fast, out_proj, out_grad):
    tokens_here = queries.shape[0]
    heads_here = gate_fast.shape[0]
    head_size = gate_fast.shape[2]
    seq_count = lax.axis_size("seq")
    seq_index = lax.axis_index("seq")

    def split_heads(array):
        return array.reshape(tokens_here, heads_here, head_size).transpose(1, 0, 2)

    def join_heads(array):
        return array.transpose(1, 0, 2).reshape(tokens_here, heads_here * head_size)

    grad_full = lax.all_gather(out_grad, "head", axis=1, tiled=True)
    out_cot = lax.dot_general(
        grad_full,
        lax.all_gather(out_proj, "seq", axis=1, tiled=True),
        (((1,), (1,)), ((), ())),
        preferred_element_type=jnp.float32,
    )
    weights = (gate_fast, up_fast, down_fast)
    scales = tuple((0.3 * math.sqrt(matrix.shape[1]) for matrix in weights))
    share_rows = [matrix.shape[1] // seq_count for matrix in weights]

    def update_heads(gate_matrix, up_matrix, down_matrix, key_heads, value_heads):
        return jax.vmap(update_terms)(
            gate_matrix, up_matrix, down_matrix, key_heads, value_heads, rates
        )

    partials, update_pull = jax.vjp(
        update_heads, gate_fast, up_fast, down_fast, split_heads(keys), split_heads(values)
    )
    totals = lax.psum((partials[0], partials[1], partials[2]), "seq")
    normed = [
        renorm(
            weights[slot],
            totals[slot],
            jnp.sum(totals[slot] * totals[slot], axis=(1, 2)),
            scales[slot],
        )
        for slot in range(3)
    ]
    renormed = [normed[slot][0] for slot in range(3)]
    new_norms = [normed[slot][1] for slot in range(3)]
    update_norms = [normed[slot][2] for slot in range(3)]

    def apply_heads(gate_matrix, up_matrix, down_matrix, query_heads):
        return jax.vmap(swiglu)(gate_matrix, up_matrix, down_matrix, query_heads)

    _, apply_pull = jax.vjp(
        apply_heads, renormed[0], renormed[1], renormed[2], split_heads(queries)
    )
    cot_gate, cot_up, cot_down, query_part = apply_pull(split_heads(out_cot))
    summed = lax.psum((cot_gate, cot_up, cot_down), "seq")
    backs = [
        back_rows(
            weights[slot],
            renormed[slot],
            new_norms[slot],
            summed[slot],
            update_norms[slot],
            scales[slot],
        )
        for slot in range(3)
    ]
    directions = [
        step_back(
            backs[slot][1],
            backs[slot][2],
            jnp.sum(backs[slot][2] * backs[slot][1], axis=(1, 2)),
            update_norms[slot],
            scales[slot],
        )
        for slot in range(3)
    ]
    directs = [
        lax.dynamic_slice_in_dim(backs[slot][0], seq_index * share_rows[slot], share_rows[slot], 1)
        for slot in range(3)
    ]
    through_gate, through_up, through_down, key_part, value_part = update_pull(
        (directions[0], directions[1], directions[2])
    )
    throughs = (
        lax.psum_scatter(through_gate, "seq", scatter_dimension=1, tiled=True),
        lax.psum_scatter(through_up, "seq", scatter_dimension=1, tiled=True),
        lax.psum_scatter(through_down, "seq", scatter_dimension=1, tiled=True),
    )
    return (
        join_heads(query_part),
        join_heads(key_part),
        join_heads(value_part),
        directs[0] + throughs[0],
        directs[1] + throughs[1],
        directs[2] + throughs[2],
    )


OCTAVES = 240.0
LANES = 128


def split(rows):
    high = rows.astype(jnp.bfloat16)
    return high, (rows - high.astype(jnp.float32)).astype(jnp.bfloat16)


def join(*pairs, axis):
    return tuple(jnp.concatenate(side, axis=axis) for side in zip(*pairs))


def dot3(left, right, dims):
    def one(a, b):
        return lax.dot_general(a, b, (dims, ((), ())), preferred_element_type=jnp.float32)

    return one(left[0], right[0]) + (one(left[0], right[1]) + one(left[1], right[0]))


NT = ((1,), (1,))
NN = ((1,), (0,))
TN = ((0,), (0,))


def encode(*groups):
    blocks, tiles = [], []
    for rows in groups:
        top = jnp.max(jnp.abs(rows), axis=1, keepdims=True)
        scale = (top * 1.01 + 1e-30).astype(jnp.bfloat16).astype(jnp.float32)
        slope = (OCTAVES * math.log(2.0)) / scale
        code = jnp.exp(jnp.abs(rows) * slope - 0.5 * OCTAVES * math.log(2.0))
        code = jnp.where(rows < 0, -code, code).astype(jnp.bfloat16)
        blocks += [code[:, at : at + LANES] for at in range(0, rows.shape[1], LANES)]
        spread = jnp.transpose(jnp.broadcast_to(scale, (rows.shape[0], LANES)))
        tiles.append(spread[: 16 // len(groups)])
    return blocks + [jnp.concatenate(tiles, axis=0).astype(jnp.bfloat16)]


def put(ref, start, blocks):
    for block in blocks:
        ref[start : start + block.shape[0], :] = block
        start += block.shape[0]
    return start


def decode(ref, start, rows, width, groups=1):
    count = width // LANES
    tile = ref[start + groups * count * rows : start + groups * count * rows + 16, :].astype(jnp.float32)
    found = []
    for group in range(groups):
        line = tile[group * (16 // groups) : group * (16 // groups) + 1]
        scale = jnp.transpose(jnp.broadcast_to(line, (LANES, rows)))
        slope = scale * (1.0 / (OCTAVES * math.log(2.0)))
        half = scale * 0.5
        parts = []
        for block in range(count):
            at = start + (group * count + block) * rows
            code = ref[at : at + rows, :].astype(jnp.float32)
            size = jnp.log(jnp.abs(code)) * slope + half
            parts.append(jnp.where(code < 0, -size, size))
        found.append(jnp.concatenate(parts, axis=1))
    return found


def coded_rows(rows, width, groups=1):
    return groups * (width // LANES) * rows + 16


def column(row):
    return jnp.transpose(jnp.broadcast_to(row, (LANES, row.shape[1])))[:, :1]


def silu_parts(before):
    sigma = 1.0 / (1.0 + jnp.exp(-before))
    return sigma, before * sigma, sigma * (1.0 + before * (1.0 - sigma))


def row_norm(matrix):
    return jnp.sqrt(jnp.sum(matrix * matrix, axis=1, keepdims=True) + 1e-06)


def call(kernel, shapes, *arrays, scratch=(), smem=0):
    specs = [pl.BlockSpec(memory_space=pltpu.SMEM)] * smem
    specs += [pl.BlockSpec(memory_space=pltpu.VMEM)] * (len(arrays) - smem)
    return pl.pallas_call(
        kernel,
        out_shape=[jax.ShapeDtypeStruct(shape, dtype) for shape, dtype in shapes],
        in_specs=specs,
        out_specs=[pl.BlockSpec(memory_space=pltpu.VMEM)] * len(shapes),
        scratch_shapes=list(scratch),
    )(*arrays)


def first_kernel(keys, values, rates, target, packed):
    scaled = -(column(rates[...]) * values[...])
    target[...] = scaled
    put(packed, 0, encode(keys[...], scaled))


def query_kernel(queries, down, packed, down_squares):
    put(packed, 0, encode(queries[...]))
    squares = jnp.sum(down[...] * down[...], axis=1, keepdims=True)
    down_squares[...] = jnp.transpose(jnp.broadcast_to(squares, (squares.shape[0], LANES)))[:1]


def body_hidden(queries, keys, values, rates, gate_fast, up_fast, down_fast, out_proj, out_grad):
    heads = lax.axis_size("head")
    seq_count = lax.axis_size("seq")
    depth = seq_count // 2
    place = lax.axis_index("seq")
    along_z = place // 2
    along_y = place % 2
    my_head = lax.axis_index("head")
    head_size = gate_fast.shape[2]
    hidden_size = gate_fast.shape[1]
    part = hidden_size // depth
    tokens = queries.shape[0]
    half = part // 2
    f32, bf16 = jnp.float32, jnp.bfloat16
    scales = tuple(0.3 * math.sqrt(matrix.shape[1]) for matrix in (gate_fast, up_fast, down_fast))
    size_one = coded_rows(tokens, head_size)
    size_two = coded_rows(tokens, head_size, 2)
    size_part = coded_rows(part, head_size)
    steps = range(1, depth)

    def turn(array, step):
        perm = [(s, (s + 2 * step) % seq_count) for s in range(seq_count)]
        return lax.ppermute(array, "seq", perm)

    def swap(array):
        return lax.ppermute(array, "seq", [(s, s ^ 1) for s in range(seq_count)])

    def gather_z(packed):
        return [turn(packed, step) for step in steps]

    def scatter_z(slots):
        return [turn(packed, -step) for step, packed in zip(steps, slots)]

    def sum_z(array):
        reach = 1
        while True:
            other = lax.ppermute(array, "seq", [(s, s ^ (2 * reach)) for s in range(seq_count)])
            reach *= 2
            if reach >= depth:
                return array, other
            array = array + other

    target, kv_packed = call(
        first_kernel, [((tokens, head_size), f32), ((size_two, LANES), bf16)], keys, values, rates
    )
    kv_sent = gather_z(kv_packed)

    perm = []
    for s in range(seq_count):
        z, y = divmod(s, 2)
        lane = (2 * z + z // (heads // 2)) % heads
        perm += [(s * heads + h, (2 * h + y) * heads + lane) for h in range(heads)]
    og_mine = lax.ppermute(out_grad, ("seq", "head"), perm)
    op_other = swap(out_proj)
    og_all = [og_mine] + [
        lax.ppermute(og_mine, "head", [(h, (h + step) % heads) for h in range(heads)])
        for step in range(1, heads)
    ]

    def contract_kernel(spot, mine, other, *refs):
        rows, outs, product = refs[:heads], refs[heads:-1], refs[-1]
        z, y, h = spot[0], spot[1], spot[2]
        width = mine.shape[1]
        for k in range(heads):
            first = rows[k][:, pl.ds(pl.multiple_of(y * width, width), width)]
            second = rows[k][:, pl.ds(pl.multiple_of((1 - y) * width, width), width)]
            block = lax.dot_general(first, mine[...], (NT, ((), ())), preferred_element_type=f32)
            block = block + lax.dot_general(second, other[...], (NT, ((), ())), preferred_element_type=f32)
            lane = lax.rem(h - k + heads, heads)
            source = lax.div(lane, 2) + lax.rem(lane, 2) * (heads // 2)
            slot = lax.rem(z - source + depth, depth)
            product[pl.ds(pl.multiple_of(slot * tokens, tokens), tokens), :] = block
        outs[0][...] = product[:tokens, :]
        for step in steps:
            put(outs[step], 0, encode(product[step * tokens : (step + 1) * tokens, :]))

    spot = jnp.stack([along_z, along_y, my_head]).astype(jnp.int32)
    oc_own, *oc_slots = call(
        contract_kernel,
        [((tokens, head_size), f32)] + [((size_one, LANES), bf16)] * (depth - 1),
        spot,
        out_proj,
        op_other,
        *og_all,
        scratch=[pltpu.VMEM((depth * tokens, head_size), f32)],
        smem=1,
    )
    oc_back = scatter_z(oc_slots)

    def total_kernel(own, *refs):
        sent, (total, packed) = refs[: depth - 1], refs[depth - 1 :]
        value = own[...]
        for ref in sent:
            value = value + decode(ref, 0, tokens, head_size)[0]
        total[...] = value
        put(packed, 0, encode(value))

    out_cot, oc_packed = call(
        total_kernel, [((tokens, head_size), f32), ((size_one, LANES), bf16)], oc_own, *oc_back
    )
    oc_sent = gather_z(oc_packed)
    q_packed, down_sq = call(
        query_kernel, [((size_one, LANES), bf16), ((1, head_size), f32)], queries, down_fast[0]
    )
    q_sent = gather_z(q_packed)

    start = along_z * part
    gate = lax.dynamic_slice_in_dim(gate_fast[0], start, part, 0)
    up = lax.dynamic_slice_in_dim(up_fast[0], start, part, 0)
    down = lax.dynamic_slice_in_dim(down_fast[0], start, part, 1).T
    weights = jnp.concatenate([gate, up, down], axis=0)

    def update_kernel(weight, key_own, target_own, *refs):
        sent = refs[: depth - 1]
        key_high, key_low, target_high, target_low, mids, partial, packed = refs[depth - 1 :]
        two = split(weight[: 2 * part, :])
        third = split(weight[2 * part :, :])
        sum_two = jnp.zeros((2 * part, head_size), f32)
        sum_one = jnp.zeros((part, head_size), f32)
        for slot in range(depth):
            at = slot * tokens
            if slot == 0:
                key_rows, target_rows = key_own[...], target_own[...]
            else:
                key_rows, target_rows = decode(sent[slot - 1], 0, tokens, head_size, 2)
            key_rows, target_rows = split(key_rows), split(target_rows)
            key_high[at : at + tokens, :], key_low[at : at + tokens, :] = key_rows
            target_high[at : at + tokens, :], target_low[at : at + tokens, :] = target_rows
            both = dot3(key_rows, two, NT)
            hgrad = dot3(target_rows, third, NT)
            mids[at : at + tokens, : 2 * part] = both
            mids[at : at + tokens, 2 * part :] = hgrad
            before, linear = both[:, :part], both[:, part:]
            _, act, slope = silu_parts(before)
            grads = split(jnp.concatenate([hgrad * linear * slope, hgrad * act], axis=1))
            sum_two = sum_two + dot3(grads, key_rows, TN)
            sum_one = sum_one + dot3(split(act * linear), target_rows, TN)
        partial[: 2 * part, :] = sum_two
        partial[2 * part :, :] = sum_one
        end = put(packed, 0, encode(sum_two[:part]))
        end = put(packed, end, encode(sum_two[part:]))
        put(packed, end, encode(sum_one))

    *kv_split, mids, partial_own, partial_packed = call(
        update_kernel,
        [((depth * tokens, head_size), bf16)] * 4
        + [((depth * tokens, 3 * part), f32), ((3 * part, head_size), f32), ((3 * size_part, LANES), bf16)],
        weights,
        keys,
        target,
        *kv_sent,
    )
    partial_other = swap(partial_packed)

    def add_swapped(own, packed, slot):
        return own[slot * part : (slot + 1) * part, :] + decode(packed, slot * size_part, part, head_size)[0]

    def put_sums(sums, first, second, third, rows_first, rows_second):
        sums[...] = jnp.zeros(sums.shape, f32)
        for line, value in enumerate((first, second, third)):
            sums[line : line + 1, :] = jnp.broadcast_to(value, (1, LANES))
        for block in range(head_size // LANES):
            at = slice(block * LANES, (block + 1) * LANES)
            sums[8 + 2 * block : 9 + 2 * block, :] = rows_first[:, at]
            sums[9 + 2 * block : 10 + 2 * block, :] = rows_second[:, at]

    def get_sums(near, far):
        count = head_size // LANES
        sums = near[...] + far[...]
        return (
            sums[0:1, 0:1],
            sums[1:2, 0:1],
            sums[2:3, 0:1],
            jnp.concatenate([sums[8 + 2 * b : 9 + 2 * b, :] for b in range(count)], axis=1),
            jnp.concatenate([sums[9 + 2 * b : 10 + 2 * b, :] for b in range(count)], axis=1),
        )

    sums_shape = (8 + 2 * (head_size // LANES), LANES)

    def whole_sum(value):
        return jnp.sum(jnp.sum(value, axis=0, keepdims=True), axis=1, keepdims=True)

    def sums_kernel(weight, own, packed, partial, sums):
        found = [add_swapped(own, packed, slot) for slot in range(3)]
        for slot in range(3):
            partial[slot * part : (slot + 1) * part, :] = found[slot]
        squares = jnp.sum(found[2] * found[2], axis=0, keepdims=True)
        put_sums(
            sums,
            whole_sum(found[0] * found[0]),
            whole_sum(found[1] * found[1]),
            jnp.sum(squares, axis=1, keepdims=True),
            squares,
            jnp.sum(found[2] * weight[2 * part :, :], axis=0, keepdims=True),
        )

    partial, sums_own = call(
        sums_kernel, [((3 * part, head_size), f32), (sums_shape, f32)], weights, partial_own, partial_other
    )
    sums = sum_z(sums_own)

    def updated(weight, down_squares, partial, *sums):
        *totals, sq_down, cross_down = get_sums(*sums)
        found = []
        for slot in range(3):
            norm = jnp.sqrt(totals[slot] + 1e-06)
            ratio = scales[slot] / norm
            matrix = weight[slot * part : (slot + 1) * part, :]
            grad = partial[slot * part : (slot + 1) * part, :]
            moved = matrix - grad * ratio
            if slot < 2:
                old, new = row_norm(matrix), row_norm(moved)
            else:
                square = down_squares[...]
                old = jnp.sqrt(square + 1e-06)
                square = square - 2.0 * ratio * cross_down + ratio * ratio * sq_down
                new = jnp.sqrt(jnp.maximum(square, 0.0) + 1e-06)
            found.append((matrix, grad, moved, old, new, norm))
        return found, cross_down - (scales[2] / found[2][5]) * sq_down

    def apply_kernel(weight, down_squares, partial, near, far, query_own, cot_own, *refs):
        count = depth - 1
        q_refs, oc_refs, outs = refs[:count], refs[count : 2 * count], refs[2 * count :]
        cots, packed, query_part, sent = outs[0], outs[1], outs[2], outs[3:]
        found, _ = updated(weight, down_squares, partial, near, far)
        renormed = [moved * (old / new) for _, _, moved, old, new, _ in found]
        two = split(jnp.concatenate(renormed[:2], axis=0))
        third = split(renormed[2])
        sum_two = jnp.zeros((2 * part, head_size), f32)
        sum_one = jnp.zeros((part, head_size), f32)
        for slot in reversed(range(depth)):
            if slot == 0:
                query_rows, cot_rows = query_own[...], cot_own[...]
            else:
                query_rows = decode(q_refs[slot - 1], 0, tokens, head_size)[0]
                cot_rows = decode(oc_refs[slot - 1], 0, tokens, head_size)[0]
            query_rows, cot_rows = split(query_rows), split(cot_rows)
            both = dot3(query_rows, two, NT)
            h_cot = dot3(cot_rows, third, NT)
            before, linear = both[:, :part], both[:, part:]
            _, act, slope = silu_parts(before)
            grads = split(jnp.concatenate([h_cot * linear * slope, h_cot * act], axis=1))
            sum_two = sum_two + dot3(grads, query_rows, TN)
            sum_one = sum_one + dot3(split(act * linear), cot_rows, TN)
            query_rows = dot3(grads, two, NN)
            if slot == 0:
                query_part[...] = query_rows
            else:
                put(sent[slot - 1], 0, encode(query_rows))
        cots[: 2 * part, :] = sum_two
        cots[2 * part :, :] = sum_one
        end = put(packed, 0, encode(sum_two[:part]))
        end = put(packed, end, encode(sum_two[part:]))
        put(packed, end, encode(sum_one))

    cots_own, cots_packed, query_part, *query_slots = call(
        apply_kernel,
        [((3 * part, head_size), f32), ((3 * size_part, LANES), bf16), ((tokens, head_size), f32)]
        + [((size_one, LANES), bf16)] * (depth - 1),
        weights,
        down_sq,
        partial,
        *sums,
        queries,
        out_cot,
        *q_sent,
        *oc_sent,
    )
    cots_other = swap(cots_packed)

    def moved_grad(entry, grad, along):
        _, _, moved, old, new, _ = entry
        return (old / new) * (grad - moved * (along / (new * new)))

    def inner_kernel(weight, down_squares, partial, near, far, own, packed, cots, inners):
        found, _ = updated(weight, down_squares, partial, near, far)
        totals = []
        for slot in range(3):
            grad = add_swapped(own, packed, slot)
            cots[slot * part : (slot + 1) * part, :] = grad
            if slot < 2:
                along = jnp.sum(found[slot][2] * grad, axis=1, keepdims=True)
                totals.append(-whole_sum(found[slot][1] * moved_grad(found[slot], grad, along)))
        put_sums(
            inners,
            totals[0],
            totals[1],
            jnp.zeros((1, 1), f32),
            jnp.sum(found[2][2] * grad, axis=0, keepdims=True),
            jnp.sum(found[2][1] * grad, axis=0, keepdims=True),
        )

    cots, inners_own = call(
        inner_kernel,
        [((3 * part, head_size), f32), (sums_shape, f32)],
        weights,
        down_sq,
        partial,
        *sums,
        cots_own,
        cots_other,
    )
    inners = sum_z(inners_own)

    def second_kernel(spot, weight, down_squares, partial, near, far, cots, inner_near, inner_far, mids, *refs):
        key_high, key_low, target_high, target_low = refs[:4]
        key_part, target_part, mine, other, down_part = refs[4:9]
        sent, (whole, direct_rows) = refs[9:-2], refs[-2:]
        found, moved_dot = updated(weight, down_squares, partial, near, far)
        inner_gate, inner_up, _, along_down, dot_down = get_sums(inner_near, inner_far)
        directions = []
        for slot in range(3):
            matrix, change, moved, old, new, norm = found[slot]
            grad = cots[slot * part : (slot + 1) * part, :]
            if slot < 2:
                along = jnp.sum(moved * grad, axis=1, keepdims=True)
                inner = (inner_gate, inner_up)[slot]
            else:
                along = along_down
                inner = -jnp.sum(
                    (old / new) * (dot_down - moved_dot * (along / (new * new))), axis=1, keepdims=True
                )
            back = moved_grad(found[slot], grad, along)
            direct_rows[slot * part : (slot + 1) * part, :] = back + (along / (new * old)) * matrix
            directions.append((scales[slot] / norm) * (-back - change * (inner / (norm * norm))))
        turn_two = split(jnp.concatenate(directions[:2], axis=0))
        turn_one = split(directions[2])
        key_matrix = join(turn_two, split(weight[: 2 * part, :]), axis=0)
        target_matrix = join(turn_one, split(weight[2 * part :, :]), axis=0)
        sum_two = jnp.zeros((2 * part, head_size), f32)
        sum_one = jnp.zeros((part, head_size), f32)
        for slot in reversed(range(depth)):
            at = slice(slot * tokens, (slot + 1) * tokens)
            key_rows = (key_high[at, :], key_low[at, :])
            target_rows = (target_high[at, :], target_low[at, :])
            both = dot3(key_rows, turn_two, NT)
            c_hidden = dot3(target_rows, turn_one, NT)
            c_bgrad, c_lgrad = both[:, :part], both[:, part:]
            before, linear = mids[at, :part], mids[at, part : 2 * part]
            hgrad = mids[at, 2 * part :]
            sigma, act, slope = silu_parts(before)
            bend = sigma * (1.0 - sigma) * (2.0 + before * (1.0 - 2.0 * sigma))
            c_linear = c_hidden * act + c_bgrad * hgrad * slope
            c_hgrad = c_bgrad * linear * slope + c_lgrad * act
            c_before = c_hidden * linear * slope + c_bgrad * hgrad * linear * bend + c_lgrad * hgrad * slope
            through = split(jnp.concatenate([c_before, c_linear], axis=1))
            grads = split(jnp.concatenate([hgrad * linear * slope, hgrad * act], axis=1))
            c_hgrad = split(c_hgrad)
            key_out = dot3(join(grads, through, axis=1), key_matrix, NN)
            target_out = dot3(join(split(act * linear), c_hgrad, axis=1), target_matrix, NN)
            if slot == 0:
                key_part[...] = key_out
                target_part[...] = target_out
            else:
                put(sent[slot - 1], 0, encode(key_out, target_out))
            sum_two = sum_two + dot3(through, key_rows, TN)
            sum_one = sum_one + dot3(c_hgrad, target_rows, TN)
        whole[...] = sum_two
        y = spot[1]
        near = pl.multiple_of(y * half, half)
        far = pl.multiple_of((1 - y) * half, half)
        for slot in range(2):
            rows = slice(slot * half, (slot + 1) * half)
            mine[rows, :] = whole[pl.ds(slot * part + near, half), :] + direct_rows[pl.ds(slot * part + near, half), :]
            other[rows, :] = whole[pl.ds(slot * part + far, half), :]
        keep = jnp.where(y == 0, 1.0, 0.0)
        down_part[...] = jnp.transpose(sum_one + direct_rows[2 * part :, :] * keep)

    key_part, target_part, rows_mine, rows_other, down_part, *grad_slots = call(
        second_kernel,
        [((tokens, head_size), f32)] * 2
        + [((2 * half, head_size), f32)] * 2
        + [((head_size, part), f32)]
        + [((size_two, LANES), bf16)] * (depth - 1),
        spot,
        weights,
        down_sq,
        partial,
        *sums,
        cots,
        *inners,
        mids,
        *kv_split,
        scratch=[pltpu.VMEM((2 * part, head_size), f32), pltpu.VMEM((3 * part, head_size), f32)],
        smem=1,
    )
    grad_back = scatter_z(grad_slots)
    rows_out = (rows_mine + swap(rows_other)).reshape(2, half, head_size)
    share = head_size // seq_count
    down_all = lax.all_to_all(down_part, "seq", 0, 0, tiled=True)
    down_all = down_all.reshape(depth, 2, share, part).sum(axis=1)
    down_out = down_all.transpose(1, 0, 2).reshape(share, hidden_size)

    query_back = scatter_z(query_slots)

    def query_end_kernel(own, *refs):
        value = own[...]
        for ref in refs[:-1]:
            value = value + decode(ref, 0, tokens, head_size)[0]
        refs[-1][...] = value

    (query_grad,) = call(query_end_kernel, [((tokens, head_size), f32)], query_part, *query_back)

    def end_kernel(rates, key_own, target_own, *refs):
        sent, (key_out, value_out) = refs[: depth - 1], refs[depth - 1 :]
        key_rows, target_rows = key_own[...], target_own[...]
        for ref in sent:
            key_more, target_more = decode(ref, 0, tokens, head_size, 2)
            key_rows, target_rows = key_rows + key_more, target_rows + target_more
        key_out[...] = key_rows
        value_out[...] = -(column(rates[...]) * target_rows)

    key_grad, value_grad = call(
        end_kernel, [((tokens, head_size), f32)] * 2, rates, key_part, target_part, *grad_back
    )
    return (query_grad, key_grad, value_grad, rows_out[0][None], rows_out[1][None], down_out[None])


def fits_hidden(mesh, tokens, hidden, head_size, heads):
    seq_count = mesh.shape["seq"]
    head_count = mesh.shape["head"]
    depth = seq_count // 2
    return (
        seq_count == 2 * head_count
        and heads == head_count
        and depth in (2, 4, 8)
        and tokens <= 3 * hidden
        and tokens == seq_count * LANES
        and hidden == depth * LANES
        and head_size % LANES == 0
        and head_size % (seq_count * 8) == 0
    )


def solution(mesh):
    placed = (
        P("seq", "head"),
        P("seq", "head"),
        P("seq", "head"),
        P("head", "seq"),
        P("head", None, None),
        P("head", None, None),
        P("head", None, None),
        P("head", "seq"),
        P("seq", "head"),
    )
    outs = (
        P("seq", "head"),
        P("seq", "head"),
        P("seq", "head"),
        P("head", "seq", None),
        P("head", "seq", None),
        P("head", "seq", None),
    )

    def whole(*arrays):
        hidden, head_size = arrays[4].shape[1:]
        small = fits_hidden(mesh, arrays[0].shape[0], hidden, head_size, arrays[4].shape[0])
        if not small:
            return jax.shard_map(body, mesh=mesh, in_specs=placed, out_specs=outs, check_vma=False)(*arrays)

        step = jax.shard_map(body_hidden, mesh=mesh, in_specs=placed, out_specs=outs, check_vma=False)
        return step(*arrays)

    return whole
```

```python
import math

import jax
import jax.numpy as jnp
from jax import lax
from jax.experimental import pallas as pl
from jax.experimental.pallas import tpu as pltpu
from jax.sharding import PartitionSpec as P


def matmul(left, right):
    return jnp.dot(left, right, precision=lax.Precision.HIGHEST, preferred_element_type=jnp.float32)


def swiglu(gate_matrix, up_matrix, down_matrix, inputs):
    before = matmul(inputs, gate_matrix.T)
    linear = matmul(inputs, up_matrix.T)
    hidden = jax.nn.silu(before) * linear
    return matmul(hidden, down_matrix.T)


def update_terms(gate_matrix, up_matrix, down_matrix, key_rows, value_rows, rate_rows):
    before = matmul(key_rows, gate_matrix.T)
    linear = matmul(key_rows, up_matrix.T)
    sigma = jax.nn.sigmoid(before)
    activated = before * sigma
    hidden = activated * linear
    target = -(rate_rows[:, None] * value_rows)
    term_down = matmul(target.T, hidden)
    hidden_grad = matmul(target, down_matrix)
    before_grad = hidden_grad * linear * sigma * (1.0 + before * (1.0 - sigma))
    linear_grad = hidden_grad * activated
    return (matmul(before_grad.T, key_rows), matmul(linear_grad.T, key_rows), term_down)


def renorm(weight, partial_value, total_sq, scale):
    norm_update = jnp.sqrt(total_sq + 1e-06)
    moved = weight - partial_value * (scale / norm_update)[..., None, None]
    norm_old = jnp.sqrt(jnp.sum(weight * weight, axis=-1) + 1e-06)
    norm_new = jnp.sqrt(jnp.sum(moved * moved, axis=-1) + 1e-06)
    return (moved * (norm_old / norm_new)[..., None], norm_new, norm_update)


def back_rows(weight, renormed, norm_new, grad, norm_update, scale):
    norm_old = jnp.sqrt(jnp.sum(weight * weight, axis=-1) + 1e-06)
    moved = renormed * (norm_new / norm_old)[..., None]
    partial_value = (weight - moved) * (norm_update / scale)[..., None, None]
    along = jnp.sum(moved * grad, axis=-1)
    moved_grad = (norm_old / norm_new)[..., None] * (
        grad - moved * (along / (norm_new * norm_new))[..., None]
    )
    direct = moved_grad + (along / (norm_new * norm_old))[..., None] * weight
    return (direct, -moved_grad, partial_value)


def step_back(step_grad, partial_value, inner, norm_update, scale):
    factor = inner / (norm_update * norm_update)
    return (scale / norm_update)[..., None, None] * (
        step_grad - partial_value * factor[..., None, None]
    )


def body(queries, keys, values, rates, gate_fast, up_fast, down_fast, out_proj, out_grad):
    tokens_here = queries.shape[0]
    heads_here = gate_fast.shape[0]
    head_size = gate_fast.shape[2]
    seq_count = lax.axis_size("seq")
    seq_index = lax.axis_index("seq")

    def split_heads(array):
        return array.reshape(tokens_here, heads_here, head_size).transpose(1, 0, 2)

    def join_heads(array):
        return array.transpose(1, 0, 2).reshape(tokens_here, heads_here * head_size)

    grad_full = lax.all_gather(out_grad, "head", axis=1, tiled=True)
    out_cot = lax.dot_general(
        grad_full,
        lax.all_gather(out_proj, "seq", axis=1, tiled=True),
        (((1,), (1,)), ((), ())),
        preferred_element_type=jnp.float32,
    )
    weights = (gate_fast, up_fast, down_fast)
    scales = tuple((0.3 * math.sqrt(matrix.shape[1]) for matrix in weights))
    share_rows = [matrix.shape[1] // seq_count for matrix in weights]

    def update_heads(gate_matrix, up_matrix, down_matrix, key_heads, value_heads):
        return jax.vmap(update_terms)(
            gate_matrix, up_matrix, down_matrix, key_heads, value_heads, rates
        )

    partials, update_pull = jax.vjp(
        update_heads, gate_fast, up_fast, down_fast, split_heads(keys), split_heads(values)
    )
    totals = lax.psum((partials[0], partials[1], partials[2]), "seq")
    normed = [
        renorm(
            weights[slot],
            totals[slot],
            jnp.sum(totals[slot] * totals[slot], axis=(1, 2)),
            scales[slot],
        )
        for slot in range(3)
    ]
    renormed = [normed[slot][0] for slot in range(3)]
    new_norms = [normed[slot][1] for slot in range(3)]
    update_norms = [normed[slot][2] for slot in range(3)]

    def apply_heads(gate_matrix, up_matrix, down_matrix, query_heads):
        return jax.vmap(swiglu)(gate_matrix, up_matrix, down_matrix, query_heads)

    _, apply_pull = jax.vjp(
        apply_heads, renormed[0], renormed[1], renormed[2], split_heads(queries)
    )
    cot_gate, cot_up, cot_down, query_part = apply_pull(split_heads(out_cot))
    summed = lax.psum((cot_gate, cot_up, cot_down), "seq")
    backs = [
        back_rows(
            weights[slot],
            renormed[slot],
            new_norms[slot],
            summed[slot],
            update_norms[slot],
            scales[slot],
        )
        for slot in range(3)
    ]
    directions = [
        step_back(
            backs[slot][1],
            backs[slot][2],
            jnp.sum(backs[slot][2] * backs[slot][1], axis=(1, 2)),
            update_norms[slot],
            scales[slot],
        )
        for slot in range(3)
    ]
    directs = [
        lax.dynamic_slice_in_dim(backs[slot][0], seq_index * share_rows[slot], share_rows[slot], 1)
        for slot in range(3)
    ]
    through_gate, through_up, through_down, key_part, value_part = update_pull(
        (directions[0], directions[1], directions[2])
    )
    throughs = (
        lax.psum_scatter(through_gate, "seq", scatter_dimension=1, tiled=True),
        lax.psum_scatter(through_up, "seq", scatter_dimension=1, tiled=True),
        lax.psum_scatter(through_down, "seq", scatter_dimension=1, tiled=True),
    )
    return (
        join_heads(query_part),
        join_heads(key_part),
        join_heads(value_part),
        directs[0] + throughs[0],
        directs[1] + throughs[1],
        directs[2] + throughs[2],
    )


OCTAVES = 240.0
LANES = 128


def split(rows):
    high = rows.astype(jnp.bfloat16)
    return high, (rows - high.astype(jnp.float32)).astype(jnp.bfloat16)


def join(*pairs, axis):
    return tuple(jnp.concatenate(side, axis=axis) for side in zip(*pairs))


def dot3(left, right, dims):
    def one(a, b):
        return lax.dot_general(a, b, (dims, ((), ())), preferred_element_type=jnp.float32)

    return one(left[0], right[0]) + (one(left[0], right[1]) + one(left[1], right[0]))


NT = ((1,), (1,))
NN = ((1,), (0,))
TN = ((0,), (0,))


def encode(*groups):
    blocks, tiles = [], []
    for rows in groups:
        top = jnp.max(jnp.abs(rows), axis=1, keepdims=True)
        scale = (top * 1.01 + 1e-30).astype(jnp.bfloat16).astype(jnp.float32)
        slope = (OCTAVES * math.log(2.0)) / scale
        code = jnp.exp(jnp.abs(rows) * slope - 0.5 * OCTAVES * math.log(2.0))
        code = jnp.where(rows < 0, -code, code).astype(jnp.bfloat16)
        blocks += [code[:, at : at + LANES] for at in range(0, rows.shape[1], LANES)]
        spread = jnp.transpose(jnp.broadcast_to(scale, (rows.shape[0], LANES)))
        tiles.append(spread[: 16 // len(groups)])
    return blocks + [jnp.concatenate(tiles, axis=0).astype(jnp.bfloat16)]


def put(ref, start, blocks):
    for block in blocks:
        ref[start : start + block.shape[0], :] = block
        start += block.shape[0]
    return start


def decode(ref, start, rows, width, groups=1):
    count = width // LANES
    tile = ref[start + groups * count * rows : start + groups * count * rows + 16, :].astype(jnp.float32)
    found = []
    for group in range(groups):
        line = tile[group * (16 // groups) : group * (16 // groups) + 1]
        scale = jnp.transpose(jnp.broadcast_to(line, (LANES, rows)))
        slope = scale * (1.0 / (OCTAVES * math.log(2.0)))
        half = scale * 0.5
        parts = []
        for block in range(count):
            at = start + (group * count + block) * rows
            code = ref[at : at + rows, :].astype(jnp.float32)
            size = jnp.log(jnp.abs(code)) * slope + half
            parts.append(jnp.where(code < 0, -size, size))
        found.append(jnp.concatenate(parts, axis=1))
    return found


def coded_rows(rows, width, groups=1):
    return groups * (width // LANES) * rows + 16


def column(row):
    return jnp.transpose(jnp.broadcast_to(row, (LANES, row.shape[1])))[:, :1]


def silu_parts(before):
    sigma = 1.0 / (1.0 + jnp.exp(-before))
    return sigma, before * sigma, sigma * (1.0 + before * (1.0 - sigma))


def row_norm(matrix):
    return jnp.sqrt(jnp.sum(matrix * matrix, axis=1, keepdims=True) + 1e-06)


def call(kernel, shapes, *arrays, scratch=(), smem=0):
    specs = [pl.BlockSpec(memory_space=pltpu.SMEM)] * smem
    specs += [pl.BlockSpec(memory_space=pltpu.VMEM)] * (len(arrays) - smem)
    return pl.pallas_call(
        kernel,
        out_shape=[jax.ShapeDtypeStruct(shape, dtype) for shape, dtype in shapes],
        in_specs=specs,
        out_specs=[pl.BlockSpec(memory_space=pltpu.VMEM)] * len(shapes),
        scratch_shapes=list(scratch),
    )(*arrays)


def first_kernel(keys, values, rates, target, packed):
    scaled = -(column(rates[...]) * values[...])
    target[...] = scaled
    put(packed, 0, encode(keys[...], scaled))


def body_hidden(queries, keys, values, rates, gate_fast, up_fast, down_fast, out_proj, out_grad):
    heads = lax.axis_size("head")
    seq_count = lax.axis_size("seq")
    depth = seq_count // 2
    place = lax.axis_index("seq")
    along_z = place // 2
    along_y = place % 2
    my_head = lax.axis_index("head")
    head_size = gate_fast.shape[2]
    hidden_size = gate_fast.shape[1]
    part = hidden_size // depth
    tokens = queries.shape[0]
    half = part // 2
    f32, bf16 = jnp.float32, jnp.bfloat16
    scales = tuple(0.3 * math.sqrt(matrix.shape[1]) for matrix in (gate_fast, up_fast, down_fast))
    size_one = coded_rows(tokens, head_size)
    size_two = coded_rows(tokens, head_size, 2)
    size_part = coded_rows(part, head_size)
    steps = range(1, depth)

    def across(array, step):
        return lax.ppermute(array, "seq", [(s, s ^ (2 * step)) for s in range(seq_count)])

    def swap(array):
        return lax.ppermute(array, "seq", [(s, s ^ 1) for s in range(seq_count)])

    def gather_z(packed):
        held, step = {0: packed}, depth // 2
        while step:
            for slot in sorted(held):
                held[slot ^ step] = across(held[slot], step)
            step //= 2
        return [held[slot] for slot in range(1, depth)]

    def scatter_z(slots):
        return [across(packed, step) for step, packed in zip(steps, slots)]

    def sum_over(array, hops):
        other = None
        for hop in hops:
            array = array if other is None else array + other
            other = lax.ppermute(array, "seq", [(s, s ^ hop) for s in range(seq_count)])
        return array, other

    z_hops = [2 << bit for bit in range(depth.bit_length() - 1)]

    spot = jnp.stack([along_z, along_y, my_head]).astype(jnp.int32)

    target, kv_packed = call(
        first_kernel, [((tokens, head_size), f32), ((size_two, LANES), bf16)], keys, values, rates
    )
    kv_sent = gather_z(kv_packed)

    perm = []
    for s in range(seq_count):
        z, y = divmod(s, 2)
        lane = (2 * z + z // (heads // 2)) % heads
        perm += [(s * heads + h, (2 * h + y) * heads + lane) for h in range(heads)]
    og_mine = lax.ppermute(out_grad, ("seq", "head"), perm)
    op_other = swap(out_proj)
    og_all, step = {0: og_mine}, heads // 2
    while step:
        for slot in sorted(og_all):
            og_all[slot ^ step] = lax.ppermute(og_all[slot], "head", [(h, h ^ step) for h in range(heads)])
        step //= 2
    og_all = [og_all[slot] for slot in range(heads)]

    def contract_kernel(spot, mine, other, *refs):
        rows, outs, product = refs[:heads], refs[heads:-1], refs[-1]
        z, y, h = spot[0], spot[1], spot[2]
        width = mine.shape[1]
        for k in range(heads):
            first = rows[k][:, pl.ds(pl.multiple_of(y * width, width), width)]
            second = rows[k][:, pl.ds(pl.multiple_of((1 - y) * width, width), width)]
            block = lax.dot_general(first, mine[...], (NT, ((), ())), preferred_element_type=f32)
            block = block + lax.dot_general(second, other[...], (NT, ((), ())), preferred_element_type=f32)
            lane = lax.bitwise_xor(h, k)
            source = lax.div(lane, 2) + lax.rem(lane, 2) * (heads // 2)
            slot = lax.bitwise_xor(z, source)
            product[pl.ds(pl.multiple_of(slot * tokens, tokens), tokens), :] = block
        outs[0][...] = product[:tokens, :]
        for step in steps:
            put(outs[step], 0, encode(product[step * tokens : (step + 1) * tokens, :]))

    oc_own, *oc_slots = call(
        contract_kernel,
        [((tokens, head_size), f32)] + [((size_one, LANES), bf16)] * (depth - 1),
        spot,
        out_proj,
        op_other,
        *og_all,
        scratch=[pltpu.VMEM((depth * tokens, head_size), f32)],
        smem=1,
    )
    oc_back = scatter_z(oc_slots)

    def total_kernel(own, *refs):
        sent, (total, packed) = refs[: depth - 1], refs[depth - 1 :]
        value = own[...]
        for ref in sent:
            value = value + decode(ref, 0, tokens, head_size)[0]
        total[...] = value
        put(packed, 0, encode(value))

    out_cot, oc_packed = call(
        total_kernel, [((tokens, head_size), f32), ((size_one, LANES), bf16)], oc_own, *oc_back
    )
    oc_sent = gather_z(oc_packed)

    def query_kernel(spot, queries, gate, up, down, packed, weight, down_squares):
        put(packed, 0, encode(queries[...]))
        squares = jnp.sum(down[...] * down[...], axis=1, keepdims=True)
        down_squares[...] = jnp.transpose(jnp.broadcast_to(squares, (squares.shape[0], LANES)))[:1]
        start = pl.multiple_of(spot[0] * part, part)
        weight[:part, :] = gate[pl.ds(start, part), :]
        weight[part : 2 * part, :] = up[pl.ds(start, part), :]
        weight[2 * part :, :] = jnp.transpose(down[:, pl.ds(start, part)])

    q_packed, weights, down_sq = call(
        query_kernel,
        [((size_one, LANES), bf16), ((3 * part, head_size), f32), ((1, head_size), f32)],
        spot,
        queries,
        gate_fast[0],
        up_fast[0],
        down_fast[0],
        smem=1,
    )
    q_sent = gather_z(q_packed)

    def update_kernel(weight, key_own, target_own, *refs):
        sent = refs[: depth - 1]
        key_high, key_low, target_high, target_low, mids, partial, packed = refs[depth - 1 :]
        two = split(weight[: 2 * part, :])
        third = split(weight[2 * part :, :])
        sum_two = jnp.zeros((2 * part, head_size), f32)
        sum_one = jnp.zeros((part, head_size), f32)
        for slot in range(depth):
            at = slot * tokens
            if slot == 0:
                key_rows, target_rows = key_own[...], target_own[...]
            else:
                key_rows, target_rows = decode(sent[slot - 1], 0, tokens, head_size, 2)
            key_rows, target_rows = split(key_rows), split(target_rows)
            key_high[at : at + tokens, :], key_low[at : at + tokens, :] = key_rows
            target_high[at : at + tokens, :], target_low[at : at + tokens, :] = target_rows
            both = dot3(key_rows, two, NT)
            hgrad = dot3(target_rows, third, NT)
            mids[at : at + tokens, : 2 * part] = both
            mids[at : at + tokens, 2 * part :] = hgrad
            before, linear = both[:, :part], both[:, part:]
            _, act, slope = silu_parts(before)
            grads = split(jnp.concatenate([hgrad * linear * slope, hgrad * act], axis=1))
            sum_two = sum_two + dot3(grads, key_rows, TN)
            sum_one = sum_one + dot3(split(act * linear), target_rows, TN)
        partial[: 2 * part, :] = sum_two
        partial[2 * part :, :] = sum_one
        end = put(packed, 0, encode(sum_two[:part]))
        end = put(packed, end, encode(sum_two[part:]))
        put(packed, end, encode(sum_one))

    *kv_split, mids, partial_own, partial_packed = call(
        update_kernel,
        [((depth * tokens, head_size), bf16)] * 4
        + [((depth * tokens, 3 * part), f32), ((3 * part, head_size), f32), ((3 * size_part, LANES), bf16)],
        weights,
        keys,
        target,
        *kv_sent,
    )
    partial_other = swap(partial_packed)

    def add_swapped(own, packed, slot):
        return own[slot * part : (slot + 1) * part, :] + decode(packed, slot * size_part, part, head_size)[0]

    def put_sums(sums, first, second, third, rows_first, rows_second):
        sums[...] = jnp.zeros(sums.shape, f32)
        for line, value in enumerate((first, second, third)):
            sums[line : line + 1, :] = jnp.broadcast_to(value, (1, LANES))
        for block in range(head_size // LANES):
            at = slice(block * LANES, (block + 1) * LANES)
            sums[8 + 2 * block : 9 + 2 * block, :] = rows_first[:, at]
            sums[9 + 2 * block : 10 + 2 * block, :] = rows_second[:, at]

    def get_sums(near, far):
        count = head_size // LANES
        sums = near[...] + far[...]
        return (
            sums[0:1, 0:1],
            sums[1:2, 0:1],
            sums[2:3, 0:1],
            jnp.concatenate([sums[8 + 2 * b : 9 + 2 * b, :] for b in range(count)], axis=1),
            jnp.concatenate([sums[9 + 2 * b : 10 + 2 * b, :] for b in range(count)], axis=1),
        )

    sums_shape = (8 + 2 * (head_size // LANES), LANES)

    def whole_sum(value):
        return jnp.sum(jnp.sum(value, axis=0, keepdims=True), axis=1, keepdims=True)

    def sums_kernel(weight, own, packed, partial, sums):
        found = [add_swapped(own, packed, slot) for slot in range(3)]
        for slot in range(3):
            partial[slot * part : (slot + 1) * part, :] = found[slot]
        squares = jnp.sum(found[2] * found[2], axis=0, keepdims=True)
        put_sums(
            sums,
            whole_sum(found[0] * found[0]),
            whole_sum(found[1] * found[1]),
            jnp.sum(squares, axis=1, keepdims=True),
            squares,
            jnp.sum(found[2] * weight[2 * part :, :], axis=0, keepdims=True),
        )

    partial, sums_own = call(
        sums_kernel, [((3 * part, head_size), f32), (sums_shape, f32)], weights, partial_own, partial_other
    )
    sums = sum_over(sums_own, z_hops)

    def updated(weight, down_squares, partial, *sums):
        *totals, sq_down, cross_down = get_sums(*sums)
        found = []
        for slot in range(3):
            norm = jnp.sqrt(totals[slot] + 1e-06)
            ratio = scales[slot] / norm
            matrix = weight[slot * part : (slot + 1) * part, :]
            grad = partial[slot * part : (slot + 1) * part, :]
            moved = matrix - grad * ratio
            if slot < 2:
                old, new = row_norm(matrix), row_norm(moved)
            else:
                square = down_squares[...]
                old = jnp.sqrt(square + 1e-06)
                square = square - 2.0 * ratio * cross_down + ratio * ratio * sq_down
                new = jnp.sqrt(jnp.maximum(square, 0.0) + 1e-06)
            found.append((matrix, grad, moved, old, new, norm))
        return found, cross_down - (scales[2] / found[2][5]) * sq_down

    def moved_grad(entry, grad, along):
        _, _, moved, old, new, _ = entry
        return (old / new) * (grad - moved * (along / (new * new)))

    def apply_kernel(weight, down_squares, partial, near, far, query_own, cot_own, *refs):
        count = depth - 1
        q_refs, oc_refs, outs = refs[:count], refs[count : 2 * count], refs[2 * count :]
        cots, packed, inners, grads_high, grads_low, two_high, two_low = outs
        found, _ = updated(weight, down_squares, partial, near, far)
        renormed = [moved * (old / new) for _, _, moved, old, new, _ in found]
        two = split(jnp.concatenate(renormed[:2], axis=0))
        third = split(renormed[2])
        two_high[...], two_low[...] = two
        sum_two = jnp.zeros((2 * part, head_size), f32)
        sum_one = jnp.zeros((part, head_size), f32)
        for slot in range(depth):
            at = slice(slot * tokens, (slot + 1) * tokens)
            if slot == 0:
                query_rows, cot_rows = query_own[...], cot_own[...]
            else:
                query_rows = decode(q_refs[slot - 1], 0, tokens, head_size)[0]
                cot_rows = decode(oc_refs[slot - 1], 0, tokens, head_size)[0]
            query_rows, cot_rows = split(query_rows), split(cot_rows)
            both = dot3(query_rows, two, NT)
            h_cot = dot3(cot_rows, third, NT)
            before, linear = both[:, :part], both[:, part:]
            _, act, slope = silu_parts(before)
            grads = split(jnp.concatenate([h_cot * linear * slope, h_cot * act], axis=1))
            grads_high[at, :], grads_low[at, :] = grads
            sum_two = sum_two + dot3(grads, query_rows, TN)
            sum_one = sum_one + dot3(split(act * linear), cot_rows, TN)
        cots[: 2 * part, :] = sum_two
        cots[2 * part :, :] = sum_one
        found_cots = (sum_two[:part], sum_two[part:], sum_one)
        end = 0
        for grad in found_cots:
            end = put(packed, end, encode(grad))
        totals = []
        for slot in range(2):
            grad = found_cots[slot]
            along = jnp.sum(found[slot][2] * grad, axis=1, keepdims=True)
            totals.append(-whole_sum(found[slot][1] * moved_grad(found[slot], grad, along)))
        put_sums(
            inners,
            totals[0],
            totals[1],
            jnp.zeros((1, 1), f32),
            jnp.sum(found[2][2] * sum_one, axis=0, keepdims=True),
            jnp.sum(found[2][1] * sum_one, axis=0, keepdims=True),
        )

    cots_own, cots_packed, inners_own, *query_parts = call(
        apply_kernel,
        [((3 * part, head_size), f32), ((3 * size_part, LANES), bf16), (sums_shape, f32)]
        + [((depth * tokens, 2 * part), bf16)] * 2
        + [((2 * part, head_size), bf16)] * 2,
        weights,
        down_sq,
        partial,
        *sums,
        queries,
        out_cot,
        *q_sent,
        *oc_sent,
    )
    cots_other = swap(cots_packed)
    inners = sum_over(inners_own, z_hops + [1])

    def query_back_kernel(grads_high, grads_low, two_high, two_low, query_part, *sent):
        two = (two_high[...], two_low[...])
        for slot in reversed(range(depth)):
            at = slice(slot * tokens, (slot + 1) * tokens)
            query_rows = dot3((grads_high[at, :], grads_low[at, :]), two, NN)
            if slot == 0:
                query_part[...] = query_rows
            else:
                put(sent[slot - 1], 0, encode(query_rows))

    query_part, *query_slots = call(
        query_back_kernel,
        [((tokens, head_size), f32)] + [((size_one, LANES), bf16)] * (depth - 1),
        *query_parts,
    )
    query_back = scatter_z(query_slots)

    def second_slot(rows, mids, turns, matrices):
        key_rows, target_rows = rows
        both = dot3(key_rows, turns[0], NT)
        c_hidden = dot3(target_rows, turns[1], NT)
        c_bgrad, c_lgrad = both[:, :part], both[:, part:]
        before, linear, hgrad = mids[:, :part], mids[:, part : 2 * part], mids[:, 2 * part :]
        sigma, act, slope = silu_parts(before)
        bend = sigma * (1.0 - sigma) * (2.0 + before * (1.0 - 2.0 * sigma))
        c_linear = c_hidden * act + c_bgrad * hgrad * slope
        c_hgrad = split(c_bgrad * linear * slope + c_lgrad * act)
        c_before = c_hidden * linear * slope + c_bgrad * hgrad * linear * bend + c_lgrad * hgrad * slope
        through = split(jnp.concatenate([c_before, c_linear], axis=1))
        grads = split(jnp.concatenate([hgrad * linear * slope, hgrad * act], axis=1))
        key_out = dot3(join(grads, through, axis=1), matrices[0], NN)
        target_out = dot3(join(split(act * linear), c_hgrad, axis=1), matrices[1], NN)
        return key_out, target_out, join(through, c_hgrad, axis=1)

    def second_kernel(weight, down_squares, partial, near, far, cots, packed, inner_near, inner_far, mids, *refs):
        kv, (turn_high, turn_low, directs, back_high, back_low, *sent) = refs[:4], refs[4:]
        found, moved_dot = updated(weight, down_squares, partial, near, far)
        inner_gate, inner_up, _, along_down, dot_down = get_sums(inner_near, inner_far)
        directions = []
        for slot in range(3):
            matrix, change, moved, old, new, norm = found[slot]
            grad = add_swapped(cots, packed, slot)
            if slot < 2:
                along = jnp.sum(moved * grad, axis=1, keepdims=True)
                inner = (inner_gate, inner_up)[slot]
            else:
                along = along_down
                inner = -jnp.sum(
                    (old / new) * (dot_down - moved_dot * (along / (new * new))), axis=1, keepdims=True
                )
            back = moved_grad(found[slot], grad, along)
            directs[slot * part : (slot + 1) * part, :] = back + (along / (new * old)) * matrix
            directions.append((scales[slot] / norm) * (-back - change * (inner / (norm * norm))))
        turns = split(jnp.concatenate(directions, axis=0))
        turn_high[...], turn_low[...] = turns
        steady = split(weight[...])
        first = [tuple(side[: 2 * part] for side in pair) for pair in (turns, steady)]
        third = [tuple(side[2 * part :] for side in pair) for pair in (turns, steady)]
        matrices = (join(*first, axis=0), join(*third, axis=0))
        for slot in reversed(range(1, depth)):
            at = slice(slot * tokens, (slot + 1) * tokens)
            rows = ((kv[0][at, :], kv[1][at, :]), (kv[2][at, :], kv[3][at, :]))
            key_out, target_out, kept = second_slot(rows, mids[at, :], (first[0], third[0]), matrices)
            put(sent[slot - 1], 0, encode(key_out, target_out))
            back_high[at, :], back_low[at, :] = kept

    turn_high, turn_low, directs, back_high, back_low, *grad_slots = call(
        second_kernel,
        [((3 * part, head_size), bf16)] * 2
        + [((3 * part, head_size), f32)]
        + [((depth * tokens, 3 * part), bf16)] * 2
        + [((size_two, LANES), bf16)] * (depth - 1),
        weights,
        down_sq,
        partial,
        *sums,
        cots_own,
        cots_other,
        *inners,
        mids,
        *kv_split,
    )
    grad_back = scatter_z(grad_slots)

    def through_kernel(spot, weight, mids, turn_high, turn_low, directs, back_high, back_low, *refs):
        kv, (key_part, target_part, kept_high, kept_low, down_part) = refs[:4], refs[4:]
        turns, steady = (turn_high[...], turn_low[...]), split(weight[...])
        first = [tuple(side[: 2 * part] for side in pair) for pair in (turns, steady)]
        third = [tuple(side[2 * part :] for side in pair) for pair in (turns, steady)]
        matrices = (join(*first, axis=0), join(*third, axis=0))
        own = slice(0, tokens)
        rows = ((kv[0][own, :], kv[1][own, :]), (kv[2][own, :], kv[3][own, :]))
        key_part[...], target_part[...], kept = second_slot(rows, mids[own, :], (first[0], third[0]), matrices)
        kept_high[...], kept_low[...] = kept
        total = dot3(tuple(side[:, 2 * part :] for side in kept), rows[1], TN)
        for slot in range(1, depth):
            at = slice(slot * tokens, (slot + 1) * tokens)
            kept = (back_high[at, 2 * part :], back_low[at, 2 * part :])
            total = total + dot3(kept, (kv[2][at, :], kv[3][at, :]), TN)
        keep = jnp.where(spot[1] == 0, 1.0, 0.0)
        down_part[...] = jnp.transpose(total + directs[2 * part :, :] * keep)

    key_part, target_part, kept_high, kept_low, down_part = call(
        through_kernel,
        [((tokens, head_size), f32)] * 2 + [((tokens, 3 * part), bf16)] * 2 + [((head_size, part), f32)],
        spot,
        weights,
        mids,
        turn_high,
        turn_low,
        directs,
        back_high,
        back_low,
        *kv_split,
        smem=1,
    )
    share = head_size // seq_count
    down_all = lax.all_to_all(down_part, "seq", 0, 0, tiled=True)

    def rows_kernel(spot, directs, kept_high, kept_low, back_high, back_low, key_high, key_low, mine, other, whole):
        total = jnp.zeros((2 * part, head_size), f32)
        for slot in range(depth):
            at = slice(slot * tokens, (slot + 1) * tokens)
            kept = (back_high[at, : 2 * part], back_low[at, : 2 * part])
            if slot == 0:
                kept = (kept_high[:, : 2 * part], kept_low[:, : 2 * part])
            total = total + dot3(kept, (key_high[at, :], key_low[at, :]), TN)
        whole[...] = total
        y = spot[1]
        near = pl.multiple_of(y * half, half)
        far = pl.multiple_of((1 - y) * half, half)
        for slot in range(2):
            rows = slice(slot * half, (slot + 1) * half)
            mine[rows, :] = whole[pl.ds(slot * part + near, half), :] + directs[pl.ds(slot * part + near, half), :]
        away = [whole[pl.ds(slot * part + far, half), :] for slot in range(2)]
        put(other, 0, encode(jnp.concatenate(away, axis=0)))

    rows_mine, rows_other = call(
        rows_kernel,
        [((2 * half, head_size), f32), ((size_part, LANES), bf16)],
        spot,
        directs,
        kept_high,
        kept_low,
        back_high,
        back_low,
        *kv_split[:2],
        scratch=[pltpu.VMEM((2 * part, head_size), f32)],
        smem=1,
    )
    rows_back = swap(rows_other)

    def query_end_kernel(own, *refs):
        value = own[...]
        for ref in refs[:-1]:
            value = value + decode(ref, 0, tokens, head_size)[0]
        refs[-1][...] = value

    (query_grad,) = call(query_end_kernel, [((tokens, head_size), f32)], query_part, *query_back)

    def finish_kernel(rows_mine, rows_back, down_all, gate_out, up_out, down_out):
        rows = rows_mine[...] + decode(rows_back, 0, 2 * half, head_size)[0]
        gate_out[0] = rows[:half]
        up_out[0] = rows[half:]
        for z in range(depth):
            at = 2 * z * share
            down_out[0, :, z * part : (z + 1) * part] = (
                down_all[at : at + share, :] + down_all[at + share : at + 2 * share, :]
            )

    gate_grad, up_grad, down_grad = call(
        finish_kernel,
        [((1, half, head_size), f32)] * 2 + [((1, share, hidden_size), f32)],
        rows_mine,
        rows_back,
        down_all,
    )

    def end_kernel(rates, key_own, target_own, *refs):
        sent, (key_out, value_out) = refs[: depth - 1], refs[depth - 1 :]
        key_rows, target_rows = key_own[...], target_own[...]
        for ref in sent:
            key_more, target_more = decode(ref, 0, tokens, head_size, 2)
            key_rows, target_rows = key_rows + key_more, target_rows + target_more
        key_out[...] = key_rows
        value_out[...] = -(column(rates[...]) * target_rows)

    key_grad, value_grad = call(
        end_kernel, [((tokens, head_size), f32)] * 2, rates, key_part, target_part, *grad_back
    )
    return query_grad, key_grad, value_grad, gate_grad, up_grad, down_grad


def fits_hidden(mesh, tokens, hidden, head_size, heads):
    seq_count = mesh.shape["seq"]
    head_count = mesh.shape["head"]
    depth = seq_count // 2
    return (
        seq_count == 2 * head_count
        and heads == head_count
        and depth in (2, 4, 8)
        and tokens <= 3 * hidden
        and tokens == seq_count * LANES
        and hidden == depth * LANES
        and head_size % LANES == 0
        and head_size % (seq_count * 8) == 0
    )


def solution(mesh):
    placed = (
        P("seq", "head"),
        P("seq", "head"),
        P("seq", "head"),
        P("head", "seq"),
        P("head", None, None),
        P("head", None, None),
        P("head", None, None),
        P("head", "seq"),
        P("seq", "head"),
    )
    outs = (
        P("seq", "head"),
        P("seq", "head"),
        P("seq", "head"),
        P("head", "seq", None),
        P("head", "seq", None),
        P("head", "seq", None),
    )

    def whole(*arrays):
        hidden, head_size = arrays[4].shape[1:]
        small = fits_hidden(mesh, arrays[0].shape[0], hidden, head_size, arrays[4].shape[0])
        if not small:
            return jax.shard_map(body, mesh=mesh, in_specs=placed, out_specs=outs, check_vma=False)(*arrays)

        step = jax.shard_map(body_hidden, mesh=mesh, in_specs=placed, out_specs=outs, check_vma=False)
        return step(*arrays)

    return whole
```

```python
import math

import jax
import jax.numpy as jnp
from jax import lax
from jax.experimental import pallas as pl
from jax.experimental.pallas import tpu as pltpu
from jax.sharding import PartitionSpec as P


def matmul(left, right):
    return jnp.dot(left, right, precision=lax.Precision.HIGHEST, preferred_element_type=jnp.float32)


def swiglu(gate_matrix, up_matrix, down_matrix, inputs):
    before = matmul(inputs, gate_matrix.T)
    linear = matmul(inputs, up_matrix.T)
    hidden = jax.nn.silu(before) * linear
    return matmul(hidden, down_matrix.T)


def update_terms(gate_matrix, up_matrix, down_matrix, key_rows, value_rows, rate_rows):
    before = matmul(key_rows, gate_matrix.T)
    linear = matmul(key_rows, up_matrix.T)
    sigma = jax.nn.sigmoid(before)
    activated = before * sigma
    hidden = activated * linear
    target = -(rate_rows[:, None] * value_rows)
    term_down = matmul(target.T, hidden)
    hidden_grad = matmul(target, down_matrix)
    before_grad = hidden_grad * linear * sigma * (1.0 + before * (1.0 - sigma))
    linear_grad = hidden_grad * activated
    return (matmul(before_grad.T, key_rows), matmul(linear_grad.T, key_rows), term_down)


def renorm(weight, partial_value, total_sq, scale):
    norm_update = jnp.sqrt(total_sq + 1e-06)
    moved = weight - partial_value * (scale / norm_update)[..., None, None]
    norm_old = jnp.sqrt(jnp.sum(weight * weight, axis=-1) + 1e-06)
    norm_new = jnp.sqrt(jnp.sum(moved * moved, axis=-1) + 1e-06)
    return (moved * (norm_old / norm_new)[..., None], norm_new, norm_update)


def back_rows(weight, renormed, norm_new, grad, norm_update, scale):
    norm_old = jnp.sqrt(jnp.sum(weight * weight, axis=-1) + 1e-06)
    moved = renormed * (norm_new / norm_old)[..., None]
    partial_value = (weight - moved) * (norm_update / scale)[..., None, None]
    along = jnp.sum(moved * grad, axis=-1)
    moved_grad = (norm_old / norm_new)[..., None] * (
        grad - moved * (along / (norm_new * norm_new))[..., None]
    )
    direct = moved_grad + (along / (norm_new * norm_old))[..., None] * weight
    return (direct, -moved_grad, partial_value)


def step_back(step_grad, partial_value, inner, norm_update, scale):
    factor = inner / (norm_update * norm_update)
    return (scale / norm_update)[..., None, None] * (
        step_grad - partial_value * factor[..., None, None]
    )


def body(queries, keys, values, rates, gate_fast, up_fast, down_fast, out_proj, out_grad):
    tokens_here = queries.shape[0]
    heads_here = gate_fast.shape[0]
    head_size = gate_fast.shape[2]
    seq_count = lax.axis_size("seq")
    seq_index = lax.axis_index("seq")

    def split_heads(array):
        return array.reshape(tokens_here, heads_here, head_size).transpose(1, 0, 2)

    def join_heads(array):
        return array.transpose(1, 0, 2).reshape(tokens_here, heads_here * head_size)

    grad_full = lax.all_gather(out_grad, "head", axis=1, tiled=True)
    out_cot = lax.dot_general(
        grad_full,
        lax.all_gather(out_proj, "seq", axis=1, tiled=True),
        (((1,), (1,)), ((), ())),
        preferred_element_type=jnp.float32,
    )
    weights = (gate_fast, up_fast, down_fast)
    scales = tuple((0.3 * math.sqrt(matrix.shape[1]) for matrix in weights))
    share_rows = [matrix.shape[1] // seq_count for matrix in weights]

    def update_heads(gate_matrix, up_matrix, down_matrix, key_heads, value_heads):
        return jax.vmap(update_terms)(
            gate_matrix, up_matrix, down_matrix, key_heads, value_heads, rates
        )

    partials, update_pull = jax.vjp(
        update_heads, gate_fast, up_fast, down_fast, split_heads(keys), split_heads(values)
    )
    totals = lax.psum((partials[0], partials[1], partials[2]), "seq")
    normed = [
        renorm(
            weights[slot],
            totals[slot],
            jnp.sum(totals[slot] * totals[slot], axis=(1, 2)),
            scales[slot],
        )
        for slot in range(3)
    ]
    renormed = [normed[slot][0] for slot in range(3)]
    new_norms = [normed[slot][1] for slot in range(3)]
    update_norms = [normed[slot][2] for slot in range(3)]

    def apply_heads(gate_matrix, up_matrix, down_matrix, query_heads):
        return jax.vmap(swiglu)(gate_matrix, up_matrix, down_matrix, query_heads)

    _, apply_pull = jax.vjp(
        apply_heads, renormed[0], renormed[1], renormed[2], split_heads(queries)
    )
    cot_gate, cot_up, cot_down, query_part = apply_pull(split_heads(out_cot))
    summed = lax.psum((cot_gate, cot_up, cot_down), "seq")
    backs = [
        back_rows(
            weights[slot],
            renormed[slot],
            new_norms[slot],
            summed[slot],
            update_norms[slot],
            scales[slot],
        )
        for slot in range(3)
    ]
    directions = [
        step_back(
            backs[slot][1],
            backs[slot][2],
            jnp.sum(backs[slot][2] * backs[slot][1], axis=(1, 2)),
            update_norms[slot],
            scales[slot],
        )
        for slot in range(3)
    ]
    directs = [
        lax.dynamic_slice_in_dim(backs[slot][0], seq_index * share_rows[slot], share_rows[slot], 1)
        for slot in range(3)
    ]
    through_gate, through_up, through_down, key_part, value_part = update_pull(
        (directions[0], directions[1], directions[2])
    )
    throughs = (
        lax.psum_scatter(through_gate, "seq", scatter_dimension=1, tiled=True),
        lax.psum_scatter(through_up, "seq", scatter_dimension=1, tiled=True),
        lax.psum_scatter(through_down, "seq", scatter_dimension=1, tiled=True),
    )
    return (
        join_heads(query_part),
        join_heads(key_part),
        join_heads(value_part),
        directs[0] + throughs[0],
        directs[1] + throughs[1],
        directs[2] + throughs[2],
    )


OCTAVES = 240.0
KERNEL_BYTES = 12 << 20
LANES = 128


def split(rows):
    high = rows.astype(jnp.bfloat16)
    return high, (rows - high.astype(jnp.float32)).astype(jnp.bfloat16)


def join(*pairs, axis):
    return tuple(jnp.concatenate(side, axis=axis) for side in zip(*pairs))


def dot3(left, right, dims):
    def one(a, b):
        return lax.dot_general(a, b, (dims, ((), ())), preferred_element_type=jnp.float32)

    return one(left[0], right[0]) + (one(left[0], right[1]) + one(left[1], right[0]))


NT = ((1,), (1,))
NN = ((1,), (0,))
TN = ((0,), (0,))


def encode(*groups):
    blocks, tiles = [], []
    for rows in groups:
        top = jnp.max(jnp.abs(rows), axis=1, keepdims=True)
        scale = (top * 1.01 + 1e-30).astype(jnp.bfloat16).astype(jnp.float32)
        slope = (OCTAVES * math.log(2.0)) / scale
        code = jnp.exp(jnp.abs(rows) * slope - 0.5 * OCTAVES * math.log(2.0))
        code = jnp.where(rows < 0, -code, code).astype(jnp.bfloat16)
        blocks += [code[:, at : at + LANES] for at in range(0, rows.shape[1], LANES)]
        spread = jnp.transpose(jnp.broadcast_to(scale, (rows.shape[0], LANES)))
        tiles.append(spread[: 16 // len(groups)])
    return blocks + [jnp.concatenate(tiles, axis=0).astype(jnp.bfloat16)]


def put(ref, start, blocks):
    for block in blocks:
        ref[start : start + block.shape[0], :] = block
        start += block.shape[0]
    return start


def decode(ref, start, rows, width, groups=1):
    count = width // LANES
    tile = ref[start + groups * count * rows : start + groups * count * rows + 16, :].astype(jnp.float32)
    found = []
    for group in range(groups):
        line = tile[group * (16 // groups) : group * (16 // groups) + 1]
        scale = jnp.transpose(jnp.broadcast_to(line, (LANES, rows)))
        slope = scale * (1.0 / (OCTAVES * math.log(2.0)))
        half = scale * 0.5
        parts = []
        for block in range(count):
            at = start + (group * count + block) * rows
            code = ref[at : at + rows, :].astype(jnp.float32)
            size = jnp.log(jnp.abs(code)) * slope + half
            parts.append(jnp.where(code < 0, -size, size))
        found.append(jnp.concatenate(parts, axis=1))
    return found


def coded_rows(rows, width, groups=1):
    return groups * (width // LANES) * rows + 16


def column(row):
    return jnp.transpose(jnp.broadcast_to(row, (LANES, row.shape[1])))[:, :1]


def silu_parts(before):
    sigma = 1.0 / (1.0 + jnp.exp(-before))
    return sigma, before * sigma, sigma * (1.0 + before * (1.0 - sigma))


def row_norm(matrix):
    return jnp.sqrt(jnp.sum(matrix * matrix, axis=1, keepdims=True) + 1e-06)


def call(kernel, shapes, *arrays, scratch=(), smem=0, raw=False):
    specs = [pl.BlockSpec(memory_space=pltpu.SMEM)] * smem
    specs += [pl.BlockSpec(memory_space=pltpu.VMEM)] * (len(arrays) - smem)
    if not raw:
        arrays = list(arrays[:smem]) + [
            pltpu.with_memory_space_constraint(array, pltpu.VMEM) for array in arrays[smem:]
        ]
    return pl.pallas_call(
        kernel,
        out_shape=[pltpu.VMEM(shape, dtype) for shape, dtype in shapes],
        in_specs=specs,
        out_specs=[pl.BlockSpec(memory_space=pltpu.VMEM)] * len(shapes),
        scratch_shapes=list(scratch),
        compiler_params=pltpu.CompilerParams(vmem_limit_bytes=KERNEL_BYTES),
    )(*arrays)


def first_kernel(keys, values, rates, target, packed):
    scaled = -(column(rates[...]) * values[...])
    target[...] = scaled
    put(packed, 0, encode(keys[...], scaled))


def body_hidden(queries, keys, values, rates, gate_fast, up_fast, down_fast, out_proj, out_grad):
    heads = lax.axis_size("head")
    seq_count = lax.axis_size("seq")
    depth = seq_count // 2
    place = lax.axis_index("seq")
    along_z = place // 2
    along_y = place % 2
    my_head = lax.axis_index("head")
    head_size = gate_fast.shape[2]
    hidden_size = gate_fast.shape[1]
    part = hidden_size // depth
    tokens = queries.shape[0]
    half = part // 2
    f32, bf16 = jnp.float32, jnp.bfloat16
    scales = tuple(0.3 * math.sqrt(matrix.shape[1]) for matrix in (gate_fast, up_fast, down_fast))
    size_one = coded_rows(tokens, head_size)
    size_two = coded_rows(tokens, head_size, 2)
    size_part = coded_rows(part, head_size)
    steps = range(1, depth)

    def across(array, step):
        return lax.ppermute(array, "seq", [(s, s ^ (2 * step)) for s in range(seq_count)])

    def swap(array):
        return lax.ppermute(array, "seq", [(s, s ^ 1) for s in range(seq_count)])

    def gather_z(packed):
        held, step = {0: packed}, depth // 2
        while step:
            for slot in sorted(held):
                held[slot ^ step] = across(held[slot], step)
            step //= 2
        return [held[slot] for slot in range(1, depth)]

    def scatter_z(slots):
        return [across(packed, step) for step, packed in zip(steps, slots)]

    def sum_over(array, hops):
        other = None
        for hop in hops:
            array = array if other is None else array + other
            other = lax.ppermute(array, "seq", [(s, s ^ hop) for s in range(seq_count)])
        return array, other

    z_hops = [2 << bit for bit in range(depth.bit_length() - 1)]

    spot = jnp.stack([along_z, along_y, my_head]).astype(jnp.int32)

    target, kv_packed = call(
        first_kernel, [((tokens, head_size), f32), ((size_two, LANES), bf16)], keys, values, rates, raw=True
    )
    kv_sent = gather_z(kv_packed)

    perm = []
    for s in range(seq_count):
        z, y = divmod(s, 2)
        lane = (2 * z + z // (heads // 2)) % heads
        perm += [(s * heads + h, (2 * h + y) * heads + lane) for h in range(heads)]
    og_mine = lax.ppermute(out_grad, ("seq", "head"), perm)
    op_other = swap(out_proj)
    og_all, step = {0: og_mine}, heads // 2
    while step:
        for slot in sorted(og_all):
            og_all[slot ^ step] = lax.ppermute(og_all[slot], "head", [(h, h ^ step) for h in range(heads)])
        step //= 2
    og_all = [og_all[slot] for slot in range(heads)]

    def contract_kernel(spot, mine, other, *refs):
        rows, outs, product = refs[:heads], refs[heads:-1], refs[-1]
        z, y, h = spot[0], spot[1], spot[2]
        width = mine.shape[1]
        for k in range(heads):
            first = rows[k][:, pl.ds(pl.multiple_of(y * width, width), width)]
            second = rows[k][:, pl.ds(pl.multiple_of((1 - y) * width, width), width)]
            block = lax.dot_general(first, mine[...], (NT, ((), ())), preferred_element_type=f32)
            block = block + lax.dot_general(second, other[...], (NT, ((), ())), preferred_element_type=f32)
            lane = lax.bitwise_xor(h, k)
            source = lax.div(lane, 2) + lax.rem(lane, 2) * (heads // 2)
            slot = lax.bitwise_xor(z, source)
            product[pl.ds(pl.multiple_of(slot * tokens, tokens), tokens), :] = block
        outs[0][...] = product[:tokens, :]
        for step in steps:
            put(outs[step], 0, encode(product[step * tokens : (step + 1) * tokens, :]))

    oc_own, *oc_slots = call(
        contract_kernel,
        [((tokens, head_size), f32)] + [((size_one, LANES), bf16)] * (depth - 1),
        spot,
        out_proj,
        op_other,
        *og_all,
        scratch=[pltpu.VMEM((depth * tokens, head_size), f32)],
        smem=1,
    )
    oc_back = scatter_z(oc_slots)

    def total_kernel(own, *refs):
        sent, (total, packed) = refs[: depth - 1], refs[depth - 1 :]
        value = own[...]
        for ref in sent:
            value = value + decode(ref, 0, tokens, head_size)[0]
        total[...] = value
        put(packed, 0, encode(value))

    out_cot, oc_packed = call(
        total_kernel, [((tokens, head_size), f32), ((size_one, LANES), bf16)], oc_own, *oc_back
    )
    oc_sent = gather_z(oc_packed)

    def query_kernel(spot, queries, gate, up, down, packed, weight, down_squares):
        put(packed, 0, encode(queries[...]))
        squares = jnp.sum(down[...] * down[...], axis=1, keepdims=True)
        down_squares[...] = jnp.transpose(jnp.broadcast_to(squares, (squares.shape[0], LANES)))[:1]
        start = pl.multiple_of(spot[0] * part, part)
        weight[:part, :] = gate[pl.ds(start, part), :]
        weight[part : 2 * part, :] = up[pl.ds(start, part), :]
        weight[2 * part :, :] = jnp.transpose(down[:, pl.ds(start, part)])

    q_packed, weights, down_sq = call(
        query_kernel,
        [((size_one, LANES), bf16), ((3 * part, head_size), f32), ((1, head_size), f32)],
        spot,
        queries,
        gate_fast[0],
        up_fast[0],
        down_fast[0],
        smem=1,
        raw=True,
    )
    q_sent = gather_z(q_packed)

    def update_kernel(weight, key_own, target_own, *refs):
        sent = refs[: depth - 1]
        key_high, key_low, target_high, target_low, mids, partial, packed = refs[depth - 1 :]
        two = split(weight[: 2 * part, :])
        third = split(weight[2 * part :, :])
        sum_two = jnp.zeros((2 * part, head_size), f32)
        sum_one = jnp.zeros((part, head_size), f32)
        for slot in range(depth):
            at = slot * tokens
            if slot == 0:
                key_rows, target_rows = key_own[...], target_own[...]
            else:
                key_rows, target_rows = decode(sent[slot - 1], 0, tokens, head_size, 2)
            key_rows, target_rows = split(key_rows), split(target_rows)
            key_high[at : at + tokens, :], key_low[at : at + tokens, :] = key_rows
            target_high[at : at + tokens, :], target_low[at : at + tokens, :] = target_rows
            both = dot3(key_rows, two, NT)
            hgrad = dot3(target_rows, third, NT)
            mids[at : at + tokens, : 2 * part] = both
            mids[at : at + tokens, 2 * part :] = hgrad
            before, linear = both[:, :part], both[:, part:]
            _, act, slope = silu_parts(before)
            grads = split(jnp.concatenate([hgrad * linear * slope, hgrad * act], axis=1))
            sum_two = sum_two + dot3(grads, key_rows, TN)
            sum_one = sum_one + dot3(split(act * linear), target_rows, TN)
        partial[: 2 * part, :] = sum_two
        partial[2 * part :, :] = sum_one
        end = put(packed, 0, encode(sum_two[:part]))
        end = put(packed, end, encode(sum_two[part:]))
        put(packed, end, encode(sum_one))

    *kv_split, mids, partial_own, partial_packed = call(
        update_kernel,
        [((depth * tokens, head_size), bf16)] * 4
        + [((depth * tokens, 3 * part), f32), ((3 * part, head_size), f32), ((3 * size_part, LANES), bf16)],
        weights,
        keys,
        target,
        *kv_sent,
    )
    partial_other = swap(partial_packed)

    def add_swapped(own, packed, slot):
        return own[slot * part : (slot + 1) * part, :] + decode(packed, slot * size_part, part, head_size)[0]

    def put_sums(sums, first, second, third, rows_first, rows_second):
        sums[...] = jnp.zeros(sums.shape, f32)
        for line, value in enumerate((first, second, third)):
            sums[line : line + 1, :] = jnp.broadcast_to(value, (1, LANES))
        for block in range(head_size // LANES):
            at = slice(block * LANES, (block + 1) * LANES)
            sums[8 + 2 * block : 9 + 2 * block, :] = rows_first[:, at]
            sums[9 + 2 * block : 10 + 2 * block, :] = rows_second[:, at]

    def get_sums(near, far):
        count = head_size // LANES
        sums = near[...] + far[...]
        return (
            sums[0:1, 0:1],
            sums[1:2, 0:1],
            sums[2:3, 0:1],
            jnp.concatenate([sums[8 + 2 * b : 9 + 2 * b, :] for b in range(count)], axis=1),
            jnp.concatenate([sums[9 + 2 * b : 10 + 2 * b, :] for b in range(count)], axis=1),
        )

    sums_shape = (8 + 2 * (head_size // LANES), LANES)

    def whole_sum(value):
        return jnp.sum(jnp.sum(value, axis=0, keepdims=True), axis=1, keepdims=True)

    def sums_kernel(weight, own, packed, partial, sums):
        found = [add_swapped(own, packed, slot) for slot in range(3)]
        for slot in range(3):
            partial[slot * part : (slot + 1) * part, :] = found[slot]
        squares = jnp.sum(found[2] * found[2], axis=0, keepdims=True)
        put_sums(
            sums,
            whole_sum(found[0] * found[0]),
            whole_sum(found[1] * found[1]),
            jnp.sum(squares, axis=1, keepdims=True),
            squares,
            jnp.sum(found[2] * weight[2 * part :, :], axis=0, keepdims=True),
        )

    partial, sums_own = call(
        sums_kernel, [((3 * part, head_size), f32), (sums_shape, f32)], weights, partial_own, partial_other
    )
    sums = sum_over(sums_own, z_hops)

    def updated(weight, down_squares, partial, *sums):
        *totals, sq_down, cross_down = get_sums(*sums)
        found = []
        for slot in range(3):
            norm = jnp.sqrt(totals[slot] + 1e-06)
            ratio = scales[slot] / norm
            matrix = weight[slot * part : (slot + 1) * part, :]
            grad = partial[slot * part : (slot + 1) * part, :]
            moved = matrix - grad * ratio
            if slot < 2:
                old, new = row_norm(matrix), row_norm(moved)
            else:
                square = down_squares[...]
                old = jnp.sqrt(square + 1e-06)
                square = square - 2.0 * ratio * cross_down + ratio * ratio * sq_down
                new = jnp.sqrt(jnp.maximum(square, 0.0) + 1e-06)
            found.append((matrix, grad, moved, old, new, norm))
        return found, cross_down - (scales[2] / found[2][5]) * sq_down

    def moved_grad(entry, grad, along):
        _, _, moved, old, new, _ = entry
        return (old / new) * (grad - moved * (along / (new * new)))

    def apply_kernel(weight, down_squares, partial, near, far, query_own, cot_own, *refs):
        count = depth - 1
        q_refs, oc_refs, outs = refs[:count], refs[count : 2 * count], refs[2 * count :]
        cots, packed, inners, grads_high, grads_low, two_high, two_low = outs
        found, _ = updated(weight, down_squares, partial, near, far)
        renormed = [moved * (old / new) for _, _, moved, old, new, _ in found]
        two = split(jnp.concatenate(renormed[:2], axis=0))
        third = split(renormed[2])
        two_high[...], two_low[...] = two
        sum_two = jnp.zeros((2 * part, head_size), f32)
        sum_one = jnp.zeros((part, head_size), f32)
        for slot in range(depth):
            at = slice(slot * tokens, (slot + 1) * tokens)
            if slot == 0:
                query_rows, cot_rows = query_own[...], cot_own[...]
            else:
                query_rows = decode(q_refs[slot - 1], 0, tokens, head_size)[0]
                cot_rows = decode(oc_refs[slot - 1], 0, tokens, head_size)[0]
            query_rows, cot_rows = split(query_rows), split(cot_rows)
            both = dot3(query_rows, two, NT)
            h_cot = dot3(cot_rows, third, NT)
            before, linear = both[:, :part], both[:, part:]
            _, act, slope = silu_parts(before)
            grads = split(jnp.concatenate([h_cot * linear * slope, h_cot * act], axis=1))
            grads_high[at, :], grads_low[at, :] = grads
            sum_two = sum_two + dot3(grads, query_rows, TN)
            sum_one = sum_one + dot3(split(act * linear), cot_rows, TN)
        cots[: 2 * part, :] = sum_two
        cots[2 * part :, :] = sum_one
        found_cots = (sum_two[:part], sum_two[part:], sum_one)
        end = 0
        for grad in found_cots:
            end = put(packed, end, encode(grad))
        totals = []
        for slot in range(2):
            grad = found_cots[slot]
            along = jnp.sum(found[slot][2] * grad, axis=1, keepdims=True)
            totals.append(-whole_sum(found[slot][1] * moved_grad(found[slot], grad, along)))
        put_sums(
            inners,
            totals[0],
            totals[1],
            jnp.zeros((1, 1), f32),
            jnp.sum(found[2][2] * sum_one, axis=0, keepdims=True),
            jnp.sum(found[2][1] * sum_one, axis=0, keepdims=True),
        )

    cots_own, cots_packed, inners_own, *query_parts = call(
        apply_kernel,
        [((3 * part, head_size), f32), ((3 * size_part, LANES), bf16), (sums_shape, f32)]
        + [((depth * tokens, 2 * part), bf16)] * 2
        + [((2 * part, head_size), bf16)] * 2,
        weights,
        down_sq,
        partial,
        *sums,
        queries,
        out_cot,
        *q_sent,
        *oc_sent,
    )
    cots_other = swap(cots_packed)
    inners = sum_over(inners_own, z_hops + [1])

    def query_back_kernel(grads_high, grads_low, two_high, two_low, query_part, *sent):
        two = (two_high[...], two_low[...])
        for slot in reversed(range(depth)):
            at = slice(slot * tokens, (slot + 1) * tokens)
            query_rows = dot3((grads_high[at, :], grads_low[at, :]), two, NN)
            if slot == 0:
                query_part[...] = query_rows
            else:
                put(sent[slot - 1], 0, encode(query_rows))

    query_part, *query_slots = call(
        query_back_kernel,
        [((tokens, head_size), f32)] + [((size_one, LANES), bf16)] * (depth - 1),
        *query_parts,
    )
    query_back = scatter_z(query_slots)

    def second_slot(rows, mids, turns, matrices):
        key_rows, target_rows = rows
        both = dot3(key_rows, turns[0], NT)
        c_hidden = dot3(target_rows, turns[1], NT)
        c_bgrad, c_lgrad = both[:, :part], both[:, part:]
        before, linear, hgrad = mids[:, :part], mids[:, part : 2 * part], mids[:, 2 * part :]
        sigma, act, slope = silu_parts(before)
        bend = sigma * (1.0 - sigma) * (2.0 + before * (1.0 - 2.0 * sigma))
        c_linear = c_hidden * act + c_bgrad * hgrad * slope
        c_hgrad = split(c_bgrad * linear * slope + c_lgrad * act)
        c_before = c_hidden * linear * slope + c_bgrad * hgrad * linear * bend + c_lgrad * hgrad * slope
        through = split(jnp.concatenate([c_before, c_linear], axis=1))
        grads = split(jnp.concatenate([hgrad * linear * slope, hgrad * act], axis=1))
        key_out = dot3(join(grads, through, axis=1), matrices[0], NN)
        target_out = dot3(join(split(act * linear), c_hgrad, axis=1), matrices[1], NN)
        return key_out, target_out, join(through, c_hgrad, axis=1)

    def second_kernel(weight, down_squares, partial, near, far, cots, packed, inner_near, inner_far, mids, *refs):
        kv, (turn_high, turn_low, directs, back_high, back_low, *sent) = refs[:4], refs[4:]
        found, moved_dot = updated(weight, down_squares, partial, near, far)
        inner_gate, inner_up, _, along_down, dot_down = get_sums(inner_near, inner_far)
        directions = []
        for slot in range(3):
            matrix, change, moved, old, new, norm = found[slot]
            grad = add_swapped(cots, packed, slot)
            if slot < 2:
                along = jnp.sum(moved * grad, axis=1, keepdims=True)
                inner = (inner_gate, inner_up)[slot]
            else:
                along = along_down
                inner = -jnp.sum(
                    (old / new) * (dot_down - moved_dot * (along / (new * new))), axis=1, keepdims=True
                )
            back = moved_grad(found[slot], grad, along)
            directs[slot * part : (slot + 1) * part, :] = back + (along / (new * old)) * matrix
            directions.append((scales[slot] / norm) * (-back - change * (inner / (norm * norm))))
        turns = split(jnp.concatenate(directions, axis=0))
        turn_high[...], turn_low[...] = turns
        steady = split(weight[...])
        first = [tuple(side[: 2 * part] for side in pair) for pair in (turns, steady)]
        third = [tuple(side[2 * part :] for side in pair) for pair in (turns, steady)]
        matrices = (join(*first, axis=0), join(*third, axis=0))
        for slot in reversed(range(1, depth)):
            at = slice(slot * tokens, (slot + 1) * tokens)
            rows = ((kv[0][at, :], kv[1][at, :]), (kv[2][at, :], kv[3][at, :]))
            key_out, target_out, kept = second_slot(rows, mids[at, :], (first[0], third[0]), matrices)
            put(sent[slot - 1], 0, encode(key_out, target_out))
            back_high[at, :], back_low[at, :] = kept

    turn_high, turn_low, directs, back_high, back_low, *grad_slots = call(
        second_kernel,
        [((3 * part, head_size), bf16)] * 2
        + [((3 * part, head_size), f32)]
        + [((depth * tokens, 3 * part), bf16)] * 2
        + [((size_two, LANES), bf16)] * (depth - 1),
        weights,
        down_sq,
        partial,
        *sums,
        cots_own,
        cots_other,
        *inners,
        mids,
        *kv_split,
    )
    grad_back = scatter_z(grad_slots)

    def through_kernel(spot, weight, mids, turn_high, turn_low, directs, back_high, back_low, *refs):
        kv, (key_part, target_part, kept_high, kept_low, down_part) = refs[:4], refs[4:]
        turns, steady = (turn_high[...], turn_low[...]), split(weight[...])
        first = [tuple(side[: 2 * part] for side in pair) for pair in (turns, steady)]
        third = [tuple(side[2 * part :] for side in pair) for pair in (turns, steady)]
        matrices = (join(*first, axis=0), join(*third, axis=0))
        own = slice(0, tokens)
        rows = ((kv[0][own, :], kv[1][own, :]), (kv[2][own, :], kv[3][own, :]))
        key_part[...], target_part[...], kept = second_slot(rows, mids[own, :], (first[0], third[0]), matrices)
        kept_high[...], kept_low[...] = kept
        total = dot3(tuple(side[:, 2 * part :] for side in kept), rows[1], TN)
        for slot in range(1, depth):
            at = slice(slot * tokens, (slot + 1) * tokens)
            kept = (back_high[at, 2 * part :], back_low[at, 2 * part :])
            total = total + dot3(kept, (kv[2][at, :], kv[3][at, :]), TN)
        keep = jnp.where(spot[1] == 0, 1.0, 0.0)
        down_part[...] = jnp.transpose(total + directs[2 * part :, :] * keep)

    key_part, target_part, kept_high, kept_low, down_part = call(
        through_kernel,
        [((tokens, head_size), f32)] * 2 + [((tokens, 3 * part), bf16)] * 2 + [((head_size, part), f32)],
        spot,
        weights,
        mids,
        turn_high,
        turn_low,
        directs,
        back_high,
        back_low,
        *kv_split,
        smem=1,
    )
    share = head_size // seq_count
    down_all = lax.all_to_all(down_part, "seq", 0, 0, tiled=True)

    def rows_kernel(spot, directs, kept_high, kept_low, back_high, back_low, key_high, key_low, mine, other, whole):
        total = jnp.zeros((2 * part, head_size), f32)
        for slot in range(depth):
            at = slice(slot * tokens, (slot + 1) * tokens)
            kept = (back_high[at, : 2 * part], back_low[at, : 2 * part])
            if slot == 0:
                kept = (kept_high[:, : 2 * part], kept_low[:, : 2 * part])
            total = total + dot3(kept, (key_high[at, :], key_low[at, :]), TN)
        whole[...] = total
        y = spot[1]
        near = pl.multiple_of(y * half, half)
        far = pl.multiple_of((1 - y) * half, half)
        for slot in range(2):
            rows = slice(slot * half, (slot + 1) * half)
            mine[rows, :] = whole[pl.ds(slot * part + near, half), :] + directs[pl.ds(slot * part + near, half), :]
        away = [whole[pl.ds(slot * part + far, half), :] for slot in range(2)]
        put(other, 0, encode(jnp.concatenate(away, axis=0)))

    rows_mine, rows_other = call(
        rows_kernel,
        [((2 * half, head_size), f32), ((size_part, LANES), bf16)],
        spot,
        directs,
        kept_high,
        kept_low,
        back_high,
        back_low,
        *kv_split[:2],
        scratch=[pltpu.VMEM((2 * part, head_size), f32)],
        smem=1,
    )
    rows_back = swap(rows_other)

    def query_end_kernel(own, *refs):
        value = own[...]
        for ref in refs[:-1]:
            value = value + decode(ref, 0, tokens, head_size)[0]
        refs[-1][...] = value

    (query_grad,) = call(query_end_kernel, [((tokens, head_size), f32)], query_part, *query_back)

    def finish_kernel(rows_mine, rows_back, down_all, gate_out, up_out, down_out):
        rows = rows_mine[...] + decode(rows_back, 0, 2 * half, head_size)[0]
        gate_out[0] = rows[:half]
        up_out[0] = rows[half:]
        for z in range(depth):
            at = 2 * z * share
            down_out[0, :, z * part : (z + 1) * part] = (
                down_all[at : at + share, :] + down_all[at + share : at + 2 * share, :]
            )

    gate_grad, up_grad, down_grad = call(
        finish_kernel,
        [((1, half, head_size), f32)] * 2 + [((1, share, hidden_size), f32)],
        rows_mine,
        rows_back,
        down_all,
    )

    def end_kernel(rates, key_own, target_own, *refs):
        sent, (key_out, value_out) = refs[: depth - 1], refs[depth - 1 :]
        key_rows, target_rows = key_own[...], target_own[...]
        for ref in sent:
            key_more, target_more = decode(ref, 0, tokens, head_size, 2)
            key_rows, target_rows = key_rows + key_more, target_rows + target_more
        key_out[...] = key_rows
        value_out[...] = -(column(rates[...]) * target_rows)

    key_grad, value_grad = call(
        end_kernel, [((tokens, head_size), f32)] * 2, rates, key_part, target_part, *grad_back
    )
    return query_grad, key_grad, value_grad, gate_grad, up_grad, down_grad


def fits_hidden(mesh, tokens, hidden, head_size, heads):
    seq_count = mesh.shape["seq"]
    head_count = mesh.shape["head"]
    depth = seq_count // 2
    return (
        seq_count == 2 * head_count
        and heads == head_count
        and depth in (2, 4, 8)
        and tokens <= 3 * hidden
        and tokens == seq_count * LANES
        and hidden == depth * LANES
        and head_size % LANES == 0
        and head_size % (seq_count * 8) == 0
    )


def solution(mesh):
    placed = (
        P("seq", "head"),
        P("seq", "head"),
        P("seq", "head"),
        P("head", "seq"),
        P("head", None, None),
        P("head", None, None),
        P("head", None, None),
        P("head", "seq"),
        P("seq", "head"),
    )
    outs = (
        P("seq", "head"),
        P("seq", "head"),
        P("seq", "head"),
        P("head", "seq", None),
        P("head", "seq", None),
        P("head", "seq", None),
    )

    def whole(*arrays):
        hidden, head_size = arrays[4].shape[1:]
        small = fits_hidden(mesh, arrays[0].shape[0], hidden, head_size, arrays[4].shape[0])
        if not small:
            return jax.shard_map(body, mesh=mesh, in_specs=placed, out_specs=outs, check_vma=False)(*arrays)

        step = jax.shard_map(body_hidden, mesh=mesh, in_specs=placed, out_specs=outs, check_vma=False)
        return step(*arrays)

    return whole
```

```python
import math

import jax
import jax.numpy as jnp
from jax import lax
from jax.experimental import pallas as pl
from jax.experimental.pallas import tpu as pltpu
from jax.sharding import PartitionSpec as P


def matmul(left, right):
    return jnp.dot(left, right, precision=lax.Precision.HIGHEST, preferred_element_type=jnp.float32)


def swiglu(gate_matrix, up_matrix, down_matrix, inputs):
    before = matmul(inputs, gate_matrix.T)
    linear = matmul(inputs, up_matrix.T)
    hidden = jax.nn.silu(before) * linear
    return matmul(hidden, down_matrix.T)


def update_terms(gate_matrix, up_matrix, down_matrix, key_rows, value_rows, rate_rows):
    before = matmul(key_rows, gate_matrix.T)
    linear = matmul(key_rows, up_matrix.T)
    sigma = jax.nn.sigmoid(before)
    activated = before * sigma
    hidden = activated * linear
    target = -(rate_rows[:, None] * value_rows)
    term_down = matmul(target.T, hidden)
    hidden_grad = matmul(target, down_matrix)
    before_grad = hidden_grad * linear * sigma * (1.0 + before * (1.0 - sigma))
    linear_grad = hidden_grad * activated
    return (matmul(before_grad.T, key_rows), matmul(linear_grad.T, key_rows), term_down)


def renorm(weight, partial_value, total_sq, scale):
    norm_update = jnp.sqrt(total_sq + 1e-06)
    moved = weight - partial_value * (scale / norm_update)[..., None, None]
    norm_old = jnp.sqrt(jnp.sum(weight * weight, axis=-1) + 1e-06)
    norm_new = jnp.sqrt(jnp.sum(moved * moved, axis=-1) + 1e-06)
    return (moved * (norm_old / norm_new)[..., None], norm_new, norm_update)


def back_rows(weight, renormed, norm_new, grad, norm_update, scale):
    norm_old = jnp.sqrt(jnp.sum(weight * weight, axis=-1) + 1e-06)
    moved = renormed * (norm_new / norm_old)[..., None]
    partial_value = (weight - moved) * (norm_update / scale)[..., None, None]
    along = jnp.sum(moved * grad, axis=-1)
    moved_grad = (norm_old / norm_new)[..., None] * (
        grad - moved * (along / (norm_new * norm_new))[..., None]
    )
    direct = moved_grad + (along / (norm_new * norm_old))[..., None] * weight
    return (direct, -moved_grad, partial_value)


def step_back(step_grad, partial_value, inner, norm_update, scale):
    factor = inner / (norm_update * norm_update)
    return (scale / norm_update)[..., None, None] * (
        step_grad - partial_value * factor[..., None, None]
    )


def body(queries, keys, values, rates, gate_fast, up_fast, down_fast, out_proj, out_grad):
    tokens_here = queries.shape[0]
    heads_here = gate_fast.shape[0]
    head_size = gate_fast.shape[2]
    seq_count = lax.axis_size("seq")
    seq_index = lax.axis_index("seq")

    def split_heads(array):
        return array.reshape(tokens_here, heads_here, head_size).transpose(1, 0, 2)

    def join_heads(array):
        return array.transpose(1, 0, 2).reshape(tokens_here, heads_here * head_size)

    grad_full = lax.all_gather(out_grad, "head", axis=1, tiled=True)
    out_cot = lax.dot_general(
        grad_full,
        lax.all_gather(out_proj, "seq", axis=1, tiled=True),
        (((1,), (1,)), ((), ())),
        preferred_element_type=jnp.float32,
    )
    weights = (gate_fast, up_fast, down_fast)
    scales = tuple((0.3 * math.sqrt(matrix.shape[1]) for matrix in weights))
    share_rows = [matrix.shape[1] // seq_count for matrix in weights]

    def update_heads(gate_matrix, up_matrix, down_matrix, key_heads, value_heads):
        return jax.vmap(update_terms)(
            gate_matrix, up_matrix, down_matrix, key_heads, value_heads, rates
        )

    partials, update_pull = jax.vjp(
        update_heads, gate_fast, up_fast, down_fast, split_heads(keys), split_heads(values)
    )
    totals = lax.psum((partials[0], partials[1], partials[2]), "seq")
    normed = [
        renorm(
            weights[slot],
            totals[slot],
            jnp.sum(totals[slot] * totals[slot], axis=(1, 2)),
            scales[slot],
        )
        for slot in range(3)
    ]
    renormed = [normed[slot][0] for slot in range(3)]
    new_norms = [normed[slot][1] for slot in range(3)]
    update_norms = [normed[slot][2] for slot in range(3)]

    def apply_heads(gate_matrix, up_matrix, down_matrix, query_heads):
        return jax.vmap(swiglu)(gate_matrix, up_matrix, down_matrix, query_heads)

    _, apply_pull = jax.vjp(
        apply_heads, renormed[0], renormed[1], renormed[2], split_heads(queries)
    )
    cot_gate, cot_up, cot_down, query_part = apply_pull(split_heads(out_cot))
    summed = lax.psum((cot_gate, cot_up, cot_down), "seq")
    backs = [
        back_rows(
            weights[slot],
            renormed[slot],
            new_norms[slot],
            summed[slot],
            update_norms[slot],
            scales[slot],
        )
        for slot in range(3)
    ]
    directions = [
        step_back(
            backs[slot][1],
            backs[slot][2],
            jnp.sum(backs[slot][2] * backs[slot][1], axis=(1, 2)),
            update_norms[slot],
            scales[slot],
        )
        for slot in range(3)
    ]
    directs = [
        lax.dynamic_slice_in_dim(backs[slot][0], seq_index * share_rows[slot], share_rows[slot], 1)
        for slot in range(3)
    ]
    through_gate, through_up, through_down, key_part, value_part = update_pull(
        (directions[0], directions[1], directions[2])
    )
    throughs = (
        lax.psum_scatter(through_gate, "seq", scatter_dimension=1, tiled=True),
        lax.psum_scatter(through_up, "seq", scatter_dimension=1, tiled=True),
        lax.psum_scatter(through_down, "seq", scatter_dimension=1, tiled=True),
    )
    return (
        join_heads(query_part),
        join_heads(key_part),
        join_heads(value_part),
        directs[0] + throughs[0],
        directs[1] + throughs[1],
        directs[2] + throughs[2],
    )


OCTAVES = 240.0
KERNEL_BYTES = 12 << 20
LANES = 128


def split(rows):
    high = rows.astype(jnp.bfloat16)
    return high, (rows - high.astype(jnp.float32)).astype(jnp.bfloat16)


def join(*pairs, axis):
    return tuple(jnp.concatenate(side, axis=axis) for side in zip(*pairs))


def dot3(left, right, dims):
    def one(a, b):
        return lax.dot_general(a, b, (dims, ((), ())), preferred_element_type=jnp.float32)

    return one(left[0], right[0]) + (one(left[0], right[1]) + one(left[1], right[0]))


NT = ((1,), (1,))
NN = ((1,), (0,))
TN = ((0,), (0,))


def encode(*groups):
    blocks, tiles = [], []
    for rows in groups:
        top = jnp.max(jnp.abs(rows), axis=1, keepdims=True)
        scale = (top * 1.01 + 1e-30).astype(jnp.bfloat16).astype(jnp.float32)
        slope = (OCTAVES * math.log(2.0)) / scale
        code = jnp.exp(jnp.abs(rows) * slope - 0.5 * OCTAVES * math.log(2.0))
        code = jnp.where(rows < 0, -code, code).astype(jnp.bfloat16)
        blocks += [code[:, at : at + LANES] for at in range(0, rows.shape[1], LANES)]
        spread = jnp.transpose(jnp.broadcast_to(scale, (rows.shape[0], LANES)))
        tiles.append(spread[: 16 // len(groups)])
    return blocks + [jnp.concatenate(tiles, axis=0).astype(jnp.bfloat16)]


def put(ref, start, blocks):
    for block in blocks:
        ref[start : start + block.shape[0], :] = block
        start += block.shape[0]
    return start


def decode(ref, start, rows, width, groups=1):
    count = width // LANES
    tile = ref[start + groups * count * rows : start + groups * count * rows + 16, :].astype(jnp.float32)
    found = []
    for group in range(groups):
        line = tile[group * (16 // groups) : group * (16 // groups) + 1]
        scale = jnp.transpose(jnp.broadcast_to(line, (LANES, rows)))
        slope = scale * (1.0 / (OCTAVES * math.log(2.0)))
        half = scale * 0.5
        parts = []
        for block in range(count):
            at = start + (group * count + block) * rows
            code = ref[at : at + rows, :].astype(jnp.float32)
            size = jnp.log(jnp.abs(code)) * slope + half
            parts.append(jnp.where(code < 0, -size, size))
        found.append(jnp.concatenate(parts, axis=1))
    return found


def coded_rows(rows, width, groups=1):
    return groups * (width // LANES) * rows + 16


def column(row):
    return jnp.transpose(jnp.broadcast_to(row, (LANES, row.shape[1])))[:, :1]


def silu_parts(before):
    sigma = 1.0 / (1.0 + jnp.exp(-before))
    return sigma, before * sigma, sigma * (1.0 + before * (1.0 - sigma))


def row_norm(matrix):
    return jnp.sqrt(jnp.sum(matrix * matrix, axis=1, keepdims=True) + 1e-06)


def call(kernel, shapes, *arrays, scratch=(), smem=0, raw=False, last=False):
    specs = [pl.BlockSpec(memory_space=pltpu.SMEM)] * smem
    specs += [pl.BlockSpec(memory_space=pltpu.VMEM)] * (len(arrays) - smem)
    place = pltpu.HBM if raw else pltpu.VMEM
    arrays = list(arrays[:smem]) + [
        pltpu.with_memory_space_constraint(array, place) for array in arrays[smem:]
    ]
    made = jax.ShapeDtypeStruct if last else pltpu.VMEM
    return pl.pallas_call(
        kernel,
        out_shape=[made(shape, dtype) for shape, dtype in shapes],
        in_specs=specs,
        out_specs=[pl.BlockSpec(memory_space=pltpu.VMEM)] * len(shapes),
        scratch_shapes=list(scratch),
        compiler_params=pltpu.CompilerParams(vmem_limit_bytes=KERNEL_BYTES),
    )(*arrays)


def first_kernel(keys, values, rates, target, packed):
    scaled = -(column(rates[...]) * values[...])
    target[...] = scaled
    put(packed, 0, encode(keys[...], scaled))


def body_hidden(queries, keys, values, rates, gate_fast, up_fast, down_fast, out_proj, out_grad):
    heads = lax.axis_size("head")
    seq_count = lax.axis_size("seq")
    depth = seq_count // 2
    place = lax.axis_index("seq")
    along_z = place // 2
    along_y = place % 2
    my_head = lax.axis_index("head")
    head_size = gate_fast.shape[2]
    hidden_size = gate_fast.shape[1]
    part = hidden_size // depth
    tokens = queries.shape[0]
    half = part // 2
    f32, bf16 = jnp.float32, jnp.bfloat16
    scales = tuple(0.3 * math.sqrt(matrix.shape[1]) for matrix in (gate_fast, up_fast, down_fast))
    size_one = coded_rows(tokens, head_size)
    size_two = coded_rows(tokens, head_size, 2)
    size_part = coded_rows(part, head_size)
    steps = range(1, depth)

    def across(array, step):
        return lax.ppermute(array, "seq", [(s, s ^ (2 * step)) for s in range(seq_count)])

    def swap(array):
        return lax.ppermute(array, "seq", [(s, s ^ 1) for s in range(seq_count)])

    def gather_z(packed):
        held, step = {0: packed}, depth // 2
        while step:
            for slot in sorted(held):
                held[slot ^ step] = across(held[slot], step)
            step //= 2
        return [held[slot] for slot in range(1, depth)]

    def scatter_z(slots):
        return [across(packed, step) for step, packed in zip(steps, slots)]

    def sum_over(array, hops):
        other = None
        for hop in hops:
            array = array if other is None else array + other
            other = lax.ppermute(array, "seq", [(s, s ^ hop) for s in range(seq_count)])
        return array, other

    z_hops = [2 << bit for bit in range(depth.bit_length() - 1)]

    spot = jnp.stack([along_z, along_y, my_head]).astype(jnp.int32)

    target, kv_packed = call(
        first_kernel, [((tokens, head_size), f32), ((size_two, LANES), bf16)], keys, values, rates, raw=True
    )
    kv_sent = gather_z(kv_packed)

    perm = []
    for s in range(seq_count):
        z, y = divmod(s, 2)
        lane = (2 * z + z // (heads // 2)) % heads
        perm += [(s * heads + h, (2 * h + y) * heads + lane) for h in range(heads)]
    og_mine = lax.ppermute(out_grad, ("seq", "head"), perm)
    op_other = swap(out_proj)
    og_all, step = {0: og_mine}, heads // 2
    while step:
        for slot in sorted(og_all):
            og_all[slot ^ step] = lax.ppermute(og_all[slot], "head", [(h, h ^ step) for h in range(heads)])
        step //= 2
    og_all = [og_all[slot] for slot in range(heads)]

    def contract_kernel(spot, mine, other, *refs):
        rows, outs, product = refs[:heads], refs[heads:-1], refs[-1]
        z, y, h = spot[0], spot[1], spot[2]
        width = mine.shape[1]
        for k in range(heads):
            first = rows[k][:, pl.ds(pl.multiple_of(y * width, width), width)]
            second = rows[k][:, pl.ds(pl.multiple_of((1 - y) * width, width), width)]
            block = lax.dot_general(first, mine[...], (NT, ((), ())), preferred_element_type=f32)
            block = block + lax.dot_general(second, other[...], (NT, ((), ())), preferred_element_type=f32)
            lane = lax.bitwise_xor(h, k)
            source = lax.div(lane, 2) + lax.rem(lane, 2) * (heads // 2)
            slot = lax.bitwise_xor(z, source)
            product[pl.ds(pl.multiple_of(slot * tokens, tokens), tokens), :] = block
        outs[0][...] = product[:tokens, :]
        for step in steps:
            put(outs[step], 0, encode(product[step * tokens : (step + 1) * tokens, :]))

    oc_own, *oc_slots = call(
        contract_kernel,
        [((tokens, head_size), f32)] + [((size_one, LANES), bf16)] * (depth - 1),
        spot,
        out_proj,
        op_other,
        *og_all,
        scratch=[pltpu.VMEM((depth * tokens, head_size), f32)],
        smem=1,
    )
    oc_back = scatter_z(oc_slots)

    def total_kernel(own, *refs):
        sent, (total, packed) = refs[: depth - 1], refs[depth - 1 :]
        value = own[...]
        for ref in sent:
            value = value + decode(ref, 0, tokens, head_size)[0]
        total[...] = value
        put(packed, 0, encode(value))

    out_cot, oc_packed = call(
        total_kernel, [((tokens, head_size), f32), ((size_one, LANES), bf16)], oc_own, *oc_back
    )
    oc_sent = gather_z(oc_packed)

    def query_kernel(spot, queries, gate, up, down, packed, weight, down_squares):
        put(packed, 0, encode(queries[...]))
        squares = jnp.sum(down[...] * down[...], axis=1, keepdims=True)
        down_squares[...] = jnp.transpose(jnp.broadcast_to(squares, (squares.shape[0], LANES)))[:1]
        start = pl.multiple_of(spot[0] * part, part)
        weight[:part, :] = gate[pl.ds(start, part), :]
        weight[part : 2 * part, :] = up[pl.ds(start, part), :]
        weight[2 * part :, :] = jnp.transpose(down[:, pl.ds(start, part)])

    q_packed, weights, down_sq = call(
        query_kernel,
        [((size_one, LANES), bf16), ((3 * part, head_size), f32), ((1, head_size), f32)],
        spot,
        queries,
        gate_fast[0],
        up_fast[0],
        down_fast[0],
        smem=1,
        raw=True,
    )
    q_sent = gather_z(q_packed)

    def update_kernel(weight, key_own, target_own, *refs):
        sent = refs[: depth - 1]
        key_high, key_low, target_high, target_low, mids, partial, packed = refs[depth - 1 :]
        two = split(weight[: 2 * part, :])
        third = split(weight[2 * part :, :])
        sum_two = jnp.zeros((2 * part, head_size), f32)
        sum_one = jnp.zeros((part, head_size), f32)
        for slot in range(depth):
            at = slot * tokens
            if slot == 0:
                key_rows, target_rows = key_own[...], target_own[...]
            else:
                key_rows, target_rows = decode(sent[slot - 1], 0, tokens, head_size, 2)
            key_rows, target_rows = split(key_rows), split(target_rows)
            key_high[at : at + tokens, :], key_low[at : at + tokens, :] = key_rows
            target_high[at : at + tokens, :], target_low[at : at + tokens, :] = target_rows
            both = dot3(key_rows, two, NT)
            hgrad = dot3(target_rows, third, NT)
            mids[at : at + tokens, : 2 * part] = both
            mids[at : at + tokens, 2 * part :] = hgrad
            before, linear = both[:, :part], both[:, part:]
            _, act, slope = silu_parts(before)
            grads = split(jnp.concatenate([hgrad * linear * slope, hgrad * act], axis=1))
            sum_two = sum_two + dot3(grads, key_rows, TN)
            sum_one = sum_one + dot3(split(act * linear), target_rows, TN)
        partial[: 2 * part, :] = sum_two
        partial[2 * part :, :] = sum_one
        end = put(packed, 0, encode(sum_two[:part]))
        end = put(packed, end, encode(sum_two[part:]))
        put(packed, end, encode(sum_one))

    *kv_split, mids, partial_own, partial_packed = call(
        update_kernel,
        [((depth * tokens, head_size), bf16)] * 4
        + [((depth * tokens, 3 * part), f32), ((3 * part, head_size), f32), ((3 * size_part, LANES), bf16)],
        weights,
        keys,
        target,
        *kv_sent,
    )
    partial_other = swap(partial_packed)

    def add_swapped(own, packed, slot):
        return own[slot * part : (slot + 1) * part, :] + decode(packed, slot * size_part, part, head_size)[0]

    def put_sums(sums, first, second, third, rows_first, rows_second):
        sums[...] = jnp.zeros(sums.shape, f32)
        for line, value in enumerate((first, second, third)):
            sums[line : line + 1, :] = jnp.broadcast_to(value, (1, LANES))
        for block in range(head_size // LANES):
            at = slice(block * LANES, (block + 1) * LANES)
            sums[8 + 2 * block : 9 + 2 * block, :] = rows_first[:, at]
            sums[9 + 2 * block : 10 + 2 * block, :] = rows_second[:, at]

    def get_sums(near, far):
        count = head_size // LANES
        sums = near[...] + far[...]
        return (
            sums[0:1, 0:1],
            sums[1:2, 0:1],
            sums[2:3, 0:1],
            jnp.concatenate([sums[8 + 2 * b : 9 + 2 * b, :] for b in range(count)], axis=1),
            jnp.concatenate([sums[9 + 2 * b : 10 + 2 * b, :] for b in range(count)], axis=1),
        )

    sums_shape = (8 + 2 * (head_size // LANES), LANES)

    def whole_sum(value):
        return jnp.sum(jnp.sum(value, axis=0, keepdims=True), axis=1, keepdims=True)

    def sums_kernel(weight, own, packed, partial, sums):
        found = [add_swapped(own, packed, slot) for slot in range(3)]
        for slot in range(3):
            partial[slot * part : (slot + 1) * part, :] = found[slot]
        squares = jnp.sum(found[2] * found[2], axis=0, keepdims=True)
        put_sums(
            sums,
            whole_sum(found[0] * found[0]),
            whole_sum(found[1] * found[1]),
            jnp.sum(squares, axis=1, keepdims=True),
            squares,
            jnp.sum(found[2] * weight[2 * part :, :], axis=0, keepdims=True),
        )

    partial, sums_own = call(
        sums_kernel, [((3 * part, head_size), f32), (sums_shape, f32)], weights, partial_own, partial_other
    )
    sums = sum_over(sums_own, z_hops)

    def updated(weight, down_squares, partial, *sums):
        *totals, sq_down, cross_down = get_sums(*sums)
        found = []
        for slot in range(3):
            norm = jnp.sqrt(totals[slot] + 1e-06)
            ratio = scales[slot] / norm
            matrix = weight[slot * part : (slot + 1) * part, :]
            grad = partial[slot * part : (slot + 1) * part, :]
            moved = matrix - grad * ratio
            if slot < 2:
                old, new = row_norm(matrix), row_norm(moved)
            else:
                square = down_squares[...]
                old = jnp.sqrt(square + 1e-06)
                square = square - 2.0 * ratio * cross_down + ratio * ratio * sq_down
                new = jnp.sqrt(jnp.maximum(square, 0.0) + 1e-06)
            found.append((matrix, grad, moved, old, new, norm))
        return found, cross_down - (scales[2] / found[2][5]) * sq_down

    def moved_grad(entry, grad, along):
        _, _, moved, old, new, _ = entry
        return (old / new) * (grad - moved * (along / (new * new)))

    def apply_kernel(weight, down_squares, partial, near, far, query_own, cot_own, *refs):
        count = depth - 1
        q_refs, oc_refs, outs = refs[:count], refs[count : 2 * count], refs[2 * count :]
        cots, packed, inners, grads_high, grads_low, two_high, two_low = outs
        found, _ = updated(weight, down_squares, partial, near, far)
        renormed = [moved * (old / new) for _, _, moved, old, new, _ in found]
        two = split(jnp.concatenate(renormed[:2], axis=0))
        third = split(renormed[2])
        two_high[...], two_low[...] = two
        sum_two = jnp.zeros((2 * part, head_size), f32)
        sum_one = jnp.zeros((part, head_size), f32)
        for slot in range(depth):
            at = slice(slot * tokens, (slot + 1) * tokens)
            if slot == 0:
                query_rows, cot_rows = query_own[...], cot_own[...]
            else:
                query_rows = decode(q_refs[slot - 1], 0, tokens, head_size)[0]
                cot_rows = decode(oc_refs[slot - 1], 0, tokens, head_size)[0]
            query_rows, cot_rows = split(query_rows), split(cot_rows)
            both = dot3(query_rows, two, NT)
            h_cot = dot3(cot_rows, third, NT)
            before, linear = both[:, :part], both[:, part:]
            _, act, slope = silu_parts(before)
            grads = split(jnp.concatenate([h_cot * linear * slope, h_cot * act], axis=1))
            grads_high[at, :], grads_low[at, :] = grads
            sum_two = sum_two + dot3(grads, query_rows, TN)
            sum_one = sum_one + dot3(split(act * linear), cot_rows, TN)
        cots[: 2 * part, :] = sum_two
        cots[2 * part :, :] = sum_one
        found_cots = (sum_two[:part], sum_two[part:], sum_one)
        end = 0
        for grad in found_cots:
            end = put(packed, end, encode(grad))
        totals = []
        for slot in range(2):
            grad = found_cots[slot]
            along = jnp.sum(found[slot][2] * grad, axis=1, keepdims=True)
            totals.append(-whole_sum(found[slot][1] * moved_grad(found[slot], grad, along)))
        put_sums(
            inners,
            totals[0],
            totals[1],
            jnp.zeros((1, 1), f32),
            jnp.sum(found[2][2] * sum_one, axis=0, keepdims=True),
            jnp.sum(found[2][1] * sum_one, axis=0, keepdims=True),
        )

    cots_own, cots_packed, inners_own, *query_parts = call(
        apply_kernel,
        [((3 * part, head_size), f32), ((3 * size_part, LANES), bf16), (sums_shape, f32)]
        + [((depth * tokens, 2 * part), bf16)] * 2
        + [((2 * part, head_size), bf16)] * 2,
        weights,
        down_sq,
        partial,
        *sums,
        queries,
        out_cot,
        *q_sent,
        *oc_sent,
    )
    cots_other = swap(cots_packed)
    inners = sum_over(inners_own, z_hops + [1])

    def query_back_kernel(grads_high, grads_low, two_high, two_low, query_part, *sent):
        two = (two_high[...], two_low[...])
        for slot in reversed(range(depth)):
            at = slice(slot * tokens, (slot + 1) * tokens)
            query_rows = dot3((grads_high[at, :], grads_low[at, :]), two, NN)
            if slot == 0:
                query_part[...] = query_rows
            else:
                put(sent[slot - 1], 0, encode(query_rows))

    query_part, *query_slots = call(
        query_back_kernel,
        [((tokens, head_size), f32)] + [((size_one, LANES), bf16)] * (depth - 1),
        *query_parts,
    )
    query_back = scatter_z(query_slots)

    def second_slot(rows, mids, turns, matrices):
        key_rows, target_rows = rows
        both = dot3(key_rows, turns[0], NT)
        c_hidden = dot3(target_rows, turns[1], NT)
        c_bgrad, c_lgrad = both[:, :part], both[:, part:]
        before, linear, hgrad = mids[:, :part], mids[:, part : 2 * part], mids[:, 2 * part :]
        sigma, act, slope = silu_parts(before)
        bend = sigma * (1.0 - sigma) * (2.0 + before * (1.0 - 2.0 * sigma))
        c_linear = c_hidden * act + c_bgrad * hgrad * slope
        c_hgrad = split(c_bgrad * linear * slope + c_lgrad * act)
        c_before = c_hidden * linear * slope + c_bgrad * hgrad * linear * bend + c_lgrad * hgrad * slope
        through = split(jnp.concatenate([c_before, c_linear], axis=1))
        grads = split(jnp.concatenate([hgrad * linear * slope, hgrad * act], axis=1))
        key_out = dot3(join(grads, through, axis=1), matrices[0], NN)
        target_out = dot3(join(split(act * linear), c_hgrad, axis=1), matrices[1], NN)
        return key_out, target_out, join(through, c_hgrad, axis=1)

    def second_kernel(weight, down_squares, partial, near, far, cots, packed, inner_near, inner_far, mids, *refs):
        kv, (turn_high, turn_low, directs, back_high, back_low, *sent) = refs[:4], refs[4:]
        found, moved_dot = updated(weight, down_squares, partial, near, far)
        inner_gate, inner_up, _, along_down, dot_down = get_sums(inner_near, inner_far)
        directions = []
        for slot in range(3):
            matrix, change, moved, old, new, norm = found[slot]
            grad = add_swapped(cots, packed, slot)
            if slot < 2:
                along = jnp.sum(moved * grad, axis=1, keepdims=True)
                inner = (inner_gate, inner_up)[slot]
            else:
                along = along_down
                inner = -jnp.sum(
                    (old / new) * (dot_down - moved_dot * (along / (new * new))), axis=1, keepdims=True
                )
            back = moved_grad(found[slot], grad, along)
            directs[slot * part : (slot + 1) * part, :] = back + (along / (new * old)) * matrix
            directions.append((scales[slot] / norm) * (-back - change * (inner / (norm * norm))))
        turns = split(jnp.concatenate(directions, axis=0))
        turn_high[...], turn_low[...] = turns
        steady = split(weight[...])
        first = [tuple(side[: 2 * part] for side in pair) for pair in (turns, steady)]
        third = [tuple(side[2 * part :] for side in pair) for pair in (turns, steady)]
        matrices = (join(*first, axis=0), join(*third, axis=0))
        for slot in reversed(range(1, depth)):
            at = slice(slot * tokens, (slot + 1) * tokens)
            rows = ((kv[0][at, :], kv[1][at, :]), (kv[2][at, :], kv[3][at, :]))
            key_out, target_out, kept = second_slot(rows, mids[at, :], (first[0], third[0]), matrices)
            put(sent[slot - 1], 0, encode(key_out, target_out))
            back_high[at, :], back_low[at, :] = kept

    turn_high, turn_low, directs, back_high, back_low, *grad_slots = call(
        second_kernel,
        [((3 * part, head_size), bf16)] * 2
        + [((3 * part, head_size), f32)]
        + [((depth * tokens, 3 * part), bf16)] * 2
        + [((size_two, LANES), bf16)] * (depth - 1),
        weights,
        down_sq,
        partial,
        *sums,
        cots_own,
        cots_other,
        *inners,
        mids,
        *kv_split,
    )
    grad_back = scatter_z(grad_slots)

    share = head_size // seq_count

    def through_kernel(spot, weight, mids, turn_high, turn_low, directs, back_high, back_low, *refs):
        kv, (key_part, target_part, mine, down_mine, away, whole, turned) = refs[:4], refs[4:]
        turns, steady = (turn_high[...], turn_low[...]), split(weight[...])
        first = [tuple(side[: 2 * part] for side in pair) for pair in (turns, steady)]
        third = [tuple(side[2 * part :] for side in pair) for pair in (turns, steady)]
        matrices = (join(*first, axis=0), join(*third, axis=0))
        sum_two = jnp.zeros((2 * part, head_size), f32)
        sum_one = jnp.zeros((part, head_size), f32)
        for slot in range(depth):
            at = slice(slot * tokens, (slot + 1) * tokens)
            rows = ((kv[0][at, :], kv[1][at, :]), (kv[2][at, :], kv[3][at, :]))
            if slot == 0:
                key_part[...], target_part[...], kept = second_slot(
                    rows, mids[at, :], (first[0], third[0]), matrices
                )
            else:
                kept = (back_high[at, :], back_low[at, :])
            sum_two = sum_two + dot3(tuple(side[:, : 2 * part] for side in kept), rows[0], TN)
            sum_one = sum_one + dot3(tuple(side[:, 2 * part :] for side in kept), rows[1], TN)
        whole[...] = sum_two
        turned[:head_size, :] = jnp.transpose(sum_one)
        turned[head_size:, :] = jnp.transpose(directs[2 * part :, :])
        y = spot[1]
        near = pl.multiple_of(y * half, half)
        far = pl.multiple_of((1 - y) * half, half)
        for slot in range(2):
            rows = slice(slot * half, (slot + 1) * half)
            mine[rows, :] = whole[pl.ds(slot * part + near, half), :] + directs[pl.ds(slot * part + near, half), :]
        others = [whole[pl.ds(slot * part + far, half), :] for slot in range(2)]
        end = put(away, 0, encode(jnp.concatenate(others, axis=0)))
        others = []
        for z in range(depth):
            near = pl.multiple_of((2 * z + y) * share, share)
            far = pl.multiple_of((2 * z + 1 - y) * share, share)
            down_mine[z * share : (z + 1) * share, :] = (
                turned[pl.ds(near, share), :] + turned[pl.ds(head_size + near, share), :]
            )
            others.append(turned[pl.ds(far, share), :])
        others = jnp.concatenate(others, axis=0)
        put(away, end, encode(*[others[at : at + LANES] for at in range(0, depth * share, LANES)]))

    groups = depth * share // LANES
    key_part, target_part, rows_mine, down_mine, rows_away = call(
        through_kernel,
        [((tokens, head_size), f32)] * 2
        + [((2 * half, head_size), f32), ((depth * share, part), f32)]
        + [((size_part + coded_rows(LANES, part, groups), LANES), bf16)],
        spot,
        weights,
        mids,
        turn_high,
        turn_low,
        directs,
        back_high,
        back_low,
        *kv_split,
        scratch=[pltpu.VMEM((2 * part, head_size), f32), pltpu.VMEM((2 * head_size, part), f32)],
        smem=1,
    )
    rows_back = swap(rows_away)

    def fold_kernel(spot, mine, down_mine, back, gate_rows, up_rows, down_own, *refs):
        sent, whole = refs[:-1], refs[-1]
        rows = mine[...] + decode(back, 0, 2 * half, head_size)[0]
        gate_rows[0] = rows[:half]
        up_rows[0] = rows[half:]
        whole[...] = down_mine[...] + jnp.concatenate(decode(back, size_part, LANES, part, groups), axis=0)
        for step in range(depth):
            at = pl.multiple_of(lax.bitwise_xor(spot[0], step) * share, share)
            (down_own, *sent)[step][...] = whole[pl.ds(at, share), :]

    gate_grad, up_grad, *down_slots = call(
        fold_kernel,
        [((1, half, head_size), f32)] * 2 + [((share, part), f32)] * depth,
        spot,
        rows_mine,
        down_mine,
        rows_back,
        scratch=[pltpu.VMEM((depth * share, part), f32)],
        smem=1,
    )
    down_back = scatter_z(down_slots[1:])

    def query_end_kernel(own, *refs):
        value = own[...]
        for ref in refs[:-1]:
            value = value + decode(ref, 0, tokens, head_size)[0]
        refs[-1][...] = value

    (query_grad,) = call(query_end_kernel, [((tokens, head_size), f32)], query_part, *query_back, last=True)

    def finish_kernel(spot, *refs):
        for step in range(depth):
            at = pl.multiple_of(lax.bitwise_xor(spot[0], step) * part, part)
            refs[-1][0, :, pl.ds(at, part)] = refs[step][...]

    (down_grad,) = call(
        finish_kernel, [((1, share, hidden_size), f32)], spot, down_slots[0], *down_back, smem=1, last=True
    )

    def end_kernel(rates, key_own, target_own, *refs):
        sent, (key_out, value_out) = refs[: depth - 1], refs[depth - 1 :]
        key_rows, target_rows = key_own[...], target_own[...]
        for ref in sent:
            key_more, target_more = decode(ref, 0, tokens, head_size, 2)
            key_rows, target_rows = key_rows + key_more, target_rows + target_more
        key_out[...] = key_rows
        value_out[...] = -(column(rates[...]) * target_rows)

    key_grad, value_grad = call(
        end_kernel, [((tokens, head_size), f32)] * 2, rates, key_part, target_part, *grad_back, last=True
    )
    return query_grad, key_grad, value_grad, gate_grad, up_grad, down_grad


def fits_hidden(mesh, tokens, hidden, head_size, heads):
    seq_count = mesh.shape["seq"]
    head_count = mesh.shape["head"]
    depth = seq_count // 2
    return (
        seq_count == 2 * head_count
        and heads == head_count
        and depth in (2, 4, 8)
        and tokens <= 3 * hidden
        and tokens == seq_count * LANES
        and hidden == depth * LANES
        and head_size % (2 * LANES) == 0
        and head_size % (seq_count * 8) == 0
    )


def solution(mesh):
    placed = (
        P("seq", "head"),
        P("seq", "head"),
        P("seq", "head"),
        P("head", "seq"),
        P("head", None, None),
        P("head", None, None),
        P("head", None, None),
        P("head", "seq"),
        P("seq", "head"),
    )
    outs = (
        P("seq", "head"),
        P("seq", "head"),
        P("seq", "head"),
        P("head", "seq", None),
        P("head", "seq", None),
        P("head", "seq", None),
    )

    def whole(*arrays):
        hidden, head_size = arrays[4].shape[1:]
        small = fits_hidden(mesh, arrays[0].shape[0], hidden, head_size, arrays[4].shape[0])
        if not small:
            return jax.shard_map(body, mesh=mesh, in_specs=placed, out_specs=outs, check_vma=False)(*arrays)

        step = jax.shard_map(body_hidden, mesh=mesh, in_specs=placed, out_specs=outs, check_vma=False)
        return step(*arrays)

    return whole
```
